32 devices in a mesh: strike: 8 (over y, x, core), dip: 4 (over z).
Axes of the slice: x: 2, y: 2, z: 4, core: 2. Of those that a mesh axis runs over, the one named last changes fastest.
Arguments:
- adjoint_state: float32 [9, 64, 64, 128], P(None, 'strike', 'dip'), may hold values from -6 to 6
- lame_lambda: float32 [64, 64, 128], P('strike', 'dip'), may hold values from 0.5 to 2
- lame_mu: float32 [64, 64, 128], P('strike', 'dip'), may hold values from 0.3 to 1.5
- buoyancy: float32 [64, 64, 128], P('strike', 'dip'), may hold values from 0.5 to 2
- residual: bfloat16 [16384, 3, 128], P(('strike', 'dip')), may hold values from -6 to 6
- receiver_tile: int32 [16384, 1], P(('strike', 'dip')), may hold values from 0 to 31; in each aligned block of 512 rows (0 to 511, 512 to 1023, ...) at most 32 rows name the same one
- receiver_cell: int32 [16384], P(('strike', 'dip')), may hold values from 0 to 16383, as said below
- resample: float32 [2, 128], replicated, may hold values from -0.5 to 0.5
- fault_patch: int32 [32, 256], P(('strike', 'dip')), may hold values from 0 to 2047, as said below
- fault_cell: int32 [32, 256], P(('strike', 'dip')), may hold values from 0 to 16383, as said below
- fault_area: float32 [32, 256], P(('strike', 'dip')), may hold values from 0.25 to 1
- moment: float32 [6, 2048], replicated, may hold values from -6 to 6
- subpatch_order: int32 [2048], replicated, may hold values from 0 to 2047, each once
Outputs:
- adjoint_out: float32 [9, 64, 64, 128], P(None, 'strike', 'dip')
- slip_gradient: float32 [2, 2048], P(None, ('strike', 'dip'))
The draws below stay inside these ranges and needn't reach their ends.
Inputs may be any that keep to these rules, and one draw needn't show every extreme that they name: `receiver_tile`: tile t is the device at index t of strike+dip. In the rows of one device at most 32 stations name the same tile. `receiver_cell`: cell of the station within the block of tile receiver_tile. `fault_patch`: the entries of tile t name subpatches within 132 of t * 64, counted cyclically. `fault_cell`: cell of the entry within the block of the tile of its row.
All inputs are finite; a program needn't handle non-finite values.
Results may differ from the reference program's by a relative error of at most 0.0003.
Values may be sent and summed in bfloat16 or wider, within the bound.
A program may use at most 64 MiB of HBM per device.

```python
import math
import jax
import jax.numpy as jnp
import numpy as np
from jax import lax

CX = 8
CY = 16
CZ = 128
STEPS = 2
NT = 128
REC_DEV = 512
SUBPATCHES = 2048
FENT = 256
TILES = 32
NX = 64
NY = 64
NZ = 128
STATIONS = 16384
SLOT = 32
SUB_OWN = 64
N_DIP = 4


def spread_cells(key, entry_count):
    cell_total = CX * CY * CZ
    values = jax.random.randint(key, (entry_count,), 0, cell_total, dtype=jnp.int32)
    anchor = jax.random.randint(jax.random.fold_in(key, 7), (), 0, entry_count, dtype=jnp.int32)
    values = values.at[anchor].set(0)
    values = values.at[(anchor + 1) % entry_count].set(cell_total - 1)
    return values


def draw_receiver_cell(key, part):
    return spread_cells(jax.random.fold_in(key, 5), STATIONS)


def draw_fault_cell(key, part):
    return spread_cells(jax.random.fold_in(key, 11), TILES * FENT).reshape(TILES, FENT)


def draw_fault_patch(key, part):
    id_spread = 2 * SUB_OWN + 4
    starts = jnp.arange(TILES, dtype=jnp.int32) * SUB_OWN
    offsets = jax.random.randint(jax.random.fold_in(key, 3), (TILES, FENT), -id_spread, id_spread + 1, dtype=jnp.int32)
    patches = (starts[:, None] + offsets) % SUBPATCHES
    patches = patches.at[:, 0].set(starts + SUB_OWN - 1)
    patches = patches.at[:, 1].set(starts)
    return patches.astype(jnp.int32)


def shard_levels(stream_key, shape, cuts, smallest, largest):
    loudness = 1.0
    for axis_at, parts in cuts:
        heights = jax.random.uniform(jax.random.fold_in(jax.random.fold_in(stream_key, 6), axis_at), (parts,), jnp.float32, smallest / len(cuts), largest / len(cuts))
        loudness = loudness * jnp.repeat(jnp.exp(heights), shape[axis_at] // parts).reshape((-1,) + (1,) * (len(shape) - 1 - axis_at))
    return loudness


def routed_block(key, own, number, rows, count, top, reach, skew):
    sequence = jax.random.permutation(key, count)
    packed, common = shares(count, rows * top, reach, skew, True), shares(count, rows * top, reach, skew, False)
    places = jnp.arange(count)

    def named(lengths, rotation):
        used = int((lengths > 0).sum())
        fixed = max(1, used // 4)
        passed = fixed + (places - fixed + rotation * (used - fixed)) % max(1, count - fixed)
        return jnp.zeros((count,), jnp.int32).at[sequence[jnp.where(places < fixed, places, passed)]].set(jnp.asarray(lengths, jnp.int32))

    lengths = jnp.where(number % 4 == 0, named(packed, number // 4), named(common, number - number // 4 - 1))
    mixed = jax.random.permutation(jax.random.fold_in(own, 3), count)
    source_of, sink = mixed[0:count // 2 * 2:2], mixed[1:count // 2 * 2:2]
    margin = jnp.minimum(lengths[source_of] - 1, reach - lengths[sink]) // 2
    margin = jnp.where((source_of == sequence[0]) | (sink == sequence[0]) | (lengths[sink] == 0), 0, jnp.maximum(margin, 0))
    passed = jax.random.randint(jax.random.fold_in(own, 4), (count // 2,), 0, 1 << 20) % (margin + 1)
    lengths = lengths.at[source_of].add(-passed).at[sink].add(passed)
    members = jnp.searchsorted(jnp.cumsum(lengths), jnp.arange(rows * top), side="right").astype(jnp.int32)
    table = members.reshape(top, rows).T
    table = table[jax.random.permutation(jax.random.fold_in(own, 1), rows)]
    rotation = jax.random.randint(jax.random.fold_in(own, 2), (rows, 1), 0, top)
    return jnp.take_along_axis(table, (jnp.arange(top)[None, :] + rotation) % top, axis=1)


def shares(amount, total, bound, slope, full):
    weights = [(1 << 20) // math.isqrt(rank ** slope) + 1 for rank in range(1, amount + 1)]
    largest = bound if full else min(bound, max(-(-total // amount), total * weights[0] // sum(weights)))
    least = 1 if total - largest >= amount - 1 else 0
    given, rest = [largest] + [least] * (amount - 1), total - largest - least * (amount - 1)
    while rest > 0:
        free = [i for i in range(1, amount) if given[i] < largest] or [i for i in range(1, amount) if given[i] < bound]
        whole, left = sum([weights[i] for i in free]), rest
        for i in free:
            more = min(bound - given[i], max(1, left * weights[i] // whole), rest)
            given[i] = given[i] + more
            rest = rest - more
    return np.array(given)


def normal_values(stream_key, shape, width, reach, shards=(), held_as=jnp.bfloat16):
    values = width * jax.random.normal(stream_key, shape, jnp.float32)
    if shards:
        values = values * shard_levels(stream_key, shape, shards, -0.22, 0.18)
    return jnp.clip(values, -reach, reach).astype(held_as)


def setup_inputs(seed: int = 0) -> dict:
    seeds = jax.random.split(jax.random.key(seed), 14)
    adjoint_state = normal_values(seeds[0], (9, NX, NY, NZ), 1.0, 6.0, ((1, 8), (2, 4)), jnp.float32)
    lame_lambda = jnp.clip(jnp.exp(math.log(2.0) - 1.3862944 * jax.random.uniform(seeds[1], (NX, NY, NZ), jnp.float32) ** shard_levels(seeds[1], (NX, NY, NZ), ((0, 8), (1, 4)), -0.2, 0.2)), 0.5, 2.0)
    lame_mu = jnp.clip(jnp.exp(math.log(1.5) - 1.60943787 * jax.random.uniform(seeds[2], (NX, NY, NZ), jnp.float32) ** shard_levels(seeds[2], (NX, NY, NZ), ((0, 8), (1, 4)), -0.2, 0.2)), 0.3, 1.5)
    buoyancy = jnp.clip(jnp.exp(math.log(2.0) - 1.3862944 * jax.random.uniform(seeds[3], (NX, NY, NZ), jnp.float32) ** shard_levels(seeds[3], (NX, NY, NZ), ((0, 8), (1, 4)), -0.2, 0.2)), 0.5, 2.0)
    residual = normal_values(seeds[4], (STATIONS, 3, NT), 1.0, 6.0, ((0, 32),))
    receiver_tile_keys = jax.random.split(jax.random.fold_in(seeds[5], 1), STATIONS // REC_DEV)
    receiver_tile_turns = jax.random.permutation(jax.random.fold_in(seeds[5], 3), STATIONS // REC_DEV)
    receiver_tile = jax.vmap(lambda own, number: routed_block(jax.random.fold_in(seeds[5], 2), own, number, REC_DEV, TILES, 1, SLOT, 2))(receiver_tile_keys, receiver_tile_turns).reshape((STATIONS, 1))
    receiver_cell = draw_receiver_cell(jax.random.fold_in(seeds[13], 71), 0)
    resample = normal_values(seeds[7], (STEPS, NT), NT ** -0.5, 0.5, (), jnp.float32)
    fault_patch = draw_fault_patch(jax.random.fold_in(seeds[13], 71), 0)
    fault_cell = draw_fault_cell(jax.random.fold_in(seeds[13], 71), 0)
    fault_area = jnp.clip(jnp.exp(math.log(1.0) - 1.3862944 * jax.random.uniform(seeds[10], (TILES, FENT), jnp.float32) ** shard_levels(seeds[10], (TILES, FENT), ((0, 32),), -0.2, 0.2)), 0.25, 1.0)
    moment = normal_values(seeds[11], (6, SUBPATCHES), 1.0, 6.0, (), jnp.float32)
    subpatch_order = jax.random.permutation(seeds[12], SUBPATCHES).astype(jnp.int32)
    return dict(adjoint_state=adjoint_state, lame_lambda=lame_lambda, lame_mu=lame_mu, buoyancy=buoyancy, residual=residual, receiver_tile=receiver_tile, receiver_cell=receiver_cell, resample=resample, fault_patch=fault_patch, fault_cell=fault_cell, fault_area=fault_area, moment=moment, subpatch_order=subpatch_order)


time_step = 0.25


def derivatives(padded):
    along_x = (padded[:, 2:, 1:-1, 1:-1] - padded[:, :-2, 1:-1, 1:-1]) * 0.5
    along_y = (padded[:, 1:-1, 2:, 1:-1] - padded[:, 1:-1, :-2, 1:-1]) * 0.5
    along_z = (padded[:, 1:-1, 1:-1, 2:] - padded[:, 1:-1, 1:-1, :-2]) * 0.5
    return along_x, along_y, along_z


def velocity_update(velocity, stress_padded, source, buoyancy):
    along_x, along_y, along_z = derivatives(stress_padded)
    force_x = along_x[0] + along_y[3] + along_z[4]
    force_y = along_x[3] + along_y[1] + along_z[5]
    force_z = along_x[4] + along_y[5] + along_z[2]
    return velocity + time_step * (buoyancy * jnp.stack([force_x, force_y, force_z]) + source)


def stress_update(stress, velocity_padded, lame_lambda, lame_mu):
    along_x, along_y, along_z = derivatives(velocity_padded)
    dilation = along_x[0] + along_y[1] + along_z[2]
    return jnp.stack([
        stress[0] + time_step * (lame_lambda * dilation + 2.0 * lame_mu * along_x[0]),
        stress[1] + time_step * (lame_lambda * dilation + 2.0 * lame_mu * along_y[1]),
        stress[2] + time_step * (lame_lambda * dilation + 2.0 * lame_mu * along_z[2]),
        stress[3] + time_step * lame_mu * (along_y[0] + along_x[1]),
        stress[4] + time_step * lame_mu * (along_z[0] + along_x[2]),
        stress[5] + time_step * lame_mu * (along_z[1] + along_y[2]),
    ])


def pad_cells(field):
    return jnp.pad(field, ((0, 0), (1, 1), (1, 1), (1, 1)))


def global_cells(tile_ids, offsets):
    strike_tile = tile_ids // N_DIP
    dip_tile = tile_ids % N_DIP
    coord_x = (strike_tile * CX + offsets // (CY * CZ)).astype(jnp.int32)
    coord_y = (dip_tile * CY + (offsets // CZ) % CY).astype(jnp.int32)
    coord_z = (offsets % CZ).astype(jnp.int32)
    return coord_x, coord_y, coord_z


def reference(adjoint_state, lame_lambda, lame_mu, buoyancy, residual, receiver_tile, receiver_cell, resample, fault_patch, fault_cell, fault_area, moment, subpatch_order):
    velocity = adjoint_state[0:3]
    stress = adjoint_state[3:9]
    amplitude = jnp.einsum("rct,kt->krc", residual.astype(jnp.float32), resample, precision=lax.Precision.HIGHEST)
    station_x, station_y, station_z = global_cells(receiver_tile[:, 0], receiver_cell)
    tile_ids = jnp.repeat(jnp.arange(TILES, dtype=jnp.int32), FENT)
    fault_x, fault_y, fault_z = global_cells(tile_ids, fault_cell.reshape(-1))
    patch_ids = fault_patch.reshape(-1)
    areas = fault_area.reshape(-1)
    pattern = moment[:, patch_ids]
    results = []
    for step in range(STEPS):
        source = jnp.zeros((3, NX, NY, NZ), jnp.float32).at[:, station_x, station_y, station_z].add(amplitude[step].T)
        velocity = velocity_update(velocity, pad_cells(stress), source, buoyancy)
        stress = stress_update(stress, pad_cells(velocity), lame_lambda, lame_mu)
        sampled = stress[:, fault_x, fault_y, fault_z]
        contrib = areas * jnp.sum(pattern * sampled, axis=0)
        partial_sum = jnp.zeros((SUBPATCHES,), jnp.float32).at[patch_ids].add(contrib)
        results.append(partial_sum[subpatch_order])
    return jnp.concatenate([velocity, stress]), jnp.stack(results)
```

```python
import functools

import jax
import jax.numpy as jnp
from jax import lax
from jax.experimental import pallas as pl
from jax.experimental.pallas import tpu as pltpu
from jax.sharding import PartitionSpec as P

LANES = 128

time_step = 0.25

MESH = pl.DeviceIdType.MESH
NT_DIMS = (((1,), (1,)), ((), ()))


def split(x):
    high = x.astype(jnp.bfloat16)
    return high, (x - high.astype(jnp.float32)).astype(jnp.bfloat16)


def one_hot(shape, axis, ids):
    return jnp.where(lax.broadcasted_iota(jnp.int32, shape, axis) == ids, 1.0, 0.0).astype(jnp.bfloat16)


def matmul(a, b):
    return jnp.dot(a, b, preferred_element_type=jnp.float32)


def matmul_nt(a, b):
    return lax.dot_general(a, b, NT_DIMS, preferred_element_type=jnp.float32)


def along_x(f, low=None, high=None):
    low = jnp.zeros_like(f[0]) if low is None else low
    high = jnp.zeros_like(f[0]) if high is None else high
    before = jnp.concatenate([low[None], f[:-1]], axis=0)
    after = jnp.concatenate([f[1:], high[None]], axis=0)
    return (after - before) * 0.5


def along_y(f, low=0.0, high=0.0):
    size = f.shape[1]
    at = lax.broadcasted_iota(jnp.int32, f.shape, 1)
    before = jnp.where(at == 0, low, pltpu.roll(f, 1, 1))
    after = jnp.where(at == size - 1, high, pltpu.roll(f, size - 1, 1))
    return (after - before) * 0.5


def along_z(f):
    size = f.shape[2]
    at = lax.broadcasted_iota(jnp.int32, f.shape, 2)
    before = jnp.where(at == 0, 0.0, pltpu.roll(f, 1, 2))
    after = jnp.where(at == size - 1, 0.0, pltpu.roll(f, size - 1, 2))
    return (after - before) * 0.5


def both(x, axis):
    return jnp.concatenate(split(x), axis=axis)


def kernel(strike_count, dip_count, slot_count, *refs):
    far, refs = refs[:13], refs[13:]
    (out, slip), refs = refs[:2], refs[2:]
    near, refs = refs[:13], refs[13:]
    state, lam, mu, buoy, residual, tiles, cells, resample, patch, fault_cell, area, moment, order = near
    steps = resample.shape[0]
    turns = steps + 1
    halves, refs = [refs[6 * t : 6 * t + 6] for t in range(turns)], refs[6 * turns :]
    (
        packed,
        landed,
        source,
        onehot_hi,
        pick,
        face_pick,
        face_weight,
        block_hot,
        lane_hot,
        corner_out,
        corner_in,
        cross_out,
        cross_in,
        sums_out,
        sums_in,
        fetch_sem,
        route_send,
        route_recv,
        halo_send,
        halo_recv,
        corner_send,
        corner_recv,
        cross_send,
        cross_recv,
        sum_send,
        sum_recv,
    ) = refs
    count = strike_count * dip_count
    strike = lax.axis_index("strike")
    dip = lax.axis_index("dip")
    me = strike * dip_count + dip
    size_x, size_y, size_z = buoy.shape
    rows = size_x * size_y
    stations = residual.shape[1]
    entries = patch.shape[1]
    shift = size_z.bit_length() - 1
    group = LANES // slot_count
    value_rows = packed.shape[1]
    owned = order.shape[1] // count
    per_block = LANES // owned
    blocks = order.shape[1] // LANES
    half = 0.5 * time_step
    slots = count * slot_count

    flip_strike = strike < strike_count // 2
    flip_dip = dip < dip_count // 2

    def turned(flip, size, k):
        return jnp.where(flip, size - 1 - k, k)

    skip = turned(flip_dip, dip_count, dip) * strike_count + turned(flip_strike, strike_count, strike)

    def each_peer(act):
        def one(n, carry):
            at = n + jnp.where(n >= skip, 1, 0)
            to_strike = turned(flip_strike, strike_count, lax.rem(at, strike_count))
            to_dip = turned(flip_dip, dip_count, at // strike_count)
            act(to_strike * dip_count + to_dip, (to_strike, to_dip))
            return carry

        lax.fori_loop(0, count - 1, one, 0)

    barrier = pltpu.get_barrier_semaphore()
    fetches = [pltpu.make_async_copy(far[i], near[i], fetch_sem.at[i]) for i in range(13)]
    early = (5, 6, 7, 4)
    for i in early:
        fetches[i].start()

    each_peer(lambda to, device: pl.semaphore_signal(barrier, inc=1, device_id=device, device_id_type=MESH))

    for i in range(13):
        if i not in early:
            fetches[i].start()

    sides = (
        (strike > 0, (strike - 1, dip)),
        (strike < strike_count - 1, (strike + 1, dip)),
        (dip > 0, (strike, dip - 1)),
        (dip < dip_count - 1, (strike, dip + 1)),
    )
    corners = tuple(
        (jnp.logical_and(sides[a][0], sides[2 + b][0]), (strike + 2 * a - 1, dip + 2 * b - 1))
        for a in range(2)
        for b in range(2)
    )

    def halo_copies(turn):
        x_out, x_low, x_high, y_out, y_low, y_high = halves[turn]
        copies = []
        for side in range(4):
            sender, low, high = (x_out, x_low, x_high) if side < 2 else (y_out, y_low, y_high)
            copies.append(
                pltpu.make_async_remote_copy(
                    src_ref=sender.at[side % 2],
                    dst_ref=high if side % 2 == 0 else low,
                    send_sem=halo_send.at[turn, side],
                    recv_sem=halo_recv.at[turn, side ^ 1],
                    device_id=sides[side][1],
                    device_id_type=MESH,
                )
            )
        return copies

    def corner_copies():
        return [
            pltpu.make_async_remote_copy(
                src_ref=corner_out.at[q],
                dst_ref=corner_in.at[3 - q],
                send_sem=corner_send.at[q],
                recv_sem=corner_recv.at[3 - q],
                device_id=corners[q][1],
                device_id_type=MESH,
            )
            for q in range(4)
        ]

    def cross_copies():
        return [
            pltpu.make_async_remote_copy(
                src_ref=cross_out.at[side],
                dst_ref=cross_in.at[side ^ 1],
                send_sem=cross_send.at[side],
                recv_sem=cross_recv.at[side ^ 1],
                device_id=sides[side][1],
                device_id_type=MESH,
            )
            for side in range(4)
        ]

    def received(turn, side):
        return halves[turn][(1, 2, 4, 5)[side]]

    def arrived(ref, sem):
        pltpu.make_async_copy(ref, ref, sem).wait()

    def stage(turn, at, x_face, y_face):
        x_out, y_out = halves[turn][0], halves[turn][3]
        for c in range(len(x_face)):
            f = x_face[c]
            x_out[0, at + c] = f[0]
            x_out[1, at + c] = f[size_x - 1]
            f = y_face[c]
            y_out[0, at + c] = f[:, 0:1]
            y_out[1, at + c] = f[:, size_y - 1 : size_y]

    def send(copies, where):
        for side, copy in enumerate(copies):
            pl.when(where[side][0])(copy.start)

    def receive(turn):
        for side in range(4):
            pl.when(sides[side][0])(functools.partial(arrived, received(turn, side), halo_recv.at[turn, side]))

    earlier = jnp.where(
        lax.broadcasted_iota(jnp.int32, (stations, stations), 0) < lax.broadcasted_iota(jnp.int32, (stations, stations), 1),
        1.0,
        0.0,
    ).astype(jnp.bfloat16)

    stress_x, stress_y = (3, 6, 7), (6, 4, 8)
    for i in early:
        fetches[i].wait()

    weights = both(resample[...] * time_step, 0)
    parts = [matmul_nt(weights, residual[c]) for c in range(3)]
    amplitude = [parts[c][k : k + 1] + parts[c][steps + k : steps + k + 1] for k in range(steps) for c in range(3)]
    cell_row = cells[...]
    hi_row = lax.shift_right_logical(cell_row, shift).astype(jnp.float32)
    lo_row = (cell_row & (size_z - 1)).astype(jnp.float32)
    values = jnp.concatenate(amplitude + [hi_row, lo_row], axis=0)
    named = one_hot((count, stations), 0, tiles[...])
    ordinal = jnp.sum(named.astype(jnp.float32) * matmul(named, earlier), axis=0, keepdims=True)
    slot_hot = lax.broadcasted_iota(jnp.int32, (slot_count, stations), 0) == ordinal.astype(jnp.int32)
    spread = []
    for r in range(value_rows):
        for part in split(values):
            pieces = [
                jnp.where(slot_hot, part[v : v + 1].astype(jnp.float32), 0.0)
                for v in range(r * group, min(8, (r + 1) * group))
            ]
            used = len(pieces) * slot_count
            if used < LANES:
                pieces.append(jnp.zeros((LANES - used, stations), jnp.float32))
            spread.append(jnp.concatenate(pieces, axis=0).astype(jnp.bfloat16))
    placed = matmul_nt(named, jnp.concatenate(spread, axis=0))
    for r in range(value_rows):
        at = 2 * r * LANES
        packed[:, r, :] = placed[:, at : at + LANES] + placed[:, at + LANES : at + 2 * LANES]

    pl.semaphore_wait(barrier, count - 1)

    def route(to, device):
        pltpu.make_async_remote_copy(
            src_ref=packed.at[to],
            dst_ref=landed.at[me],
            send_sem=route_send,
            recv_sem=route_recv,
            device_id=device,
            device_id_type=MESH,
        ).start()

    each_peer(route)
    landed[me] = packed[me]
    for i in (0, 1, 2):
        fetches[i].wait()
    stage(0, 0, [state[i] for i in stress_x], [state[i] for i in stress_y])
    stage(0, 3, [lam[...], mu[...]], [lam[...], mu[...]])
    send(halo_copies(0), sides)
    for i in range(3, 13):
        if i not in early:
            fetches[i].wait()

    for side in range(4):

        def clear(side=side):
            for turn in range(turns):
                target = received(turn, side)
                target[...] = jnp.zeros_like(target)
            cross_in[side] = jnp.zeros_like(cross_in[side])

        pl.when(jnp.logical_not(sides[side][0]))(clear)
    for q in range(4):

        def clear_corner(q=q):
            corner_in[q] = jnp.zeros_like(corner_in[q])

        pl.when(jnp.logical_not(corners[q][0]))(clear_corner)

    patch_row = patch[...]
    cell_e = fault_cell[...]
    row_e = lax.shift_right_logical(cell_e, shift)
    deep_e = cell_e & (size_z - 1)
    pick_lo = one_hot((size_z, entries), 0, deep_e)
    pick[...] = jnp.concatenate([pick_lo, pick_lo], axis=0)
    onehot_hi[...] = jnp.where(lax.broadcasted_iota(jnp.int32, (rows, entries), 0) == row_e, 1.0, 0.0)
    chosen = matmul(both(moment[...], 0), one_hot((moment.shape[1], entries), 0, patch_row))
    pattern = (chosen[:6] + chosen[6:]) * area[...]
    patch_col = jnp.transpose(jnp.broadcast_to(patch_row.astype(jnp.float32), (LANES, entries)))
    picks = jnp.concatenate(
        [
            jnp.where(patch_col == order[:, b * LANES : (b + 1) * LANES].astype(jnp.float32), 1.0, 0.0).astype(
                jnp.bfloat16
            )
            for b in range(blocks)
        ],
        axis=1,
    )
    number = lax.broadcasted_iota(jnp.int32, (8, order.shape[1]), 1)
    which = lax.broadcasted_iota(jnp.int32, (8, order.shape[1]), 0)
    number = jnp.where(which == 0, number // LANES, number % LANES).astype(jnp.float32).astype(jnp.bfloat16)
    place = matmul_nt(number, picks)[:2]

    def sampled(field):
        return matmul(both(field.reshape(rows, size_z), 1), pick[...])

    def at_entries(field):
        return jnp.sum(sampled(field) * onehot_hi[...], axis=0, keepdims=True)

    lam_e, mu_e = at_entries(lam[...]), at_entries(mu[...])
    stiff_e = lam_e + 2.0 * mu_e
    pxx, pyy, pzz, pxy, pxz, pyz = [pattern[m : m + 1] for m in range(6)]
    x_e, y_e = row_e // size_y, lax.rem(row_e, size_y)
    x_weight = (pxx * stiff_e + (pyy + pzz) * lam_e, pxy * mu_e, pxz * mu_e)
    y_weight = (pxy * mu_e, pyy * stiff_e + (pxx + pzz) * lam_e, pyz * mu_e)
    tail = [deep_e.astype(jnp.float32), place, jnp.zeros((1, entries), jnp.float32)]
    for side in range(4):
        on, across, weight = (x_e, y_e, x_weight) if side < 2 else (y_e, x_e, y_weight)
        edge = 0 if side % 2 == 0 else (size_x if side < 2 else size_y) - 1
        scale = jnp.where(on == edge, -half if side % 2 == 0 else half, 0.0)
        cross_out[side] = jnp.concatenate([w * scale for w in weight] + [across.astype(jnp.float32)] + tail, axis=0)
    send(cross_copies(), sides)

    def halo(turn, c):
        return [received(turn, side)[c] for side in range(4)]

    rhs = ((3, 6, 7), (6, 4, 8), (7, 8, 5))

    def velocity(fields, edges, extra):
        for c in range(3):
            xx, yy, zz = rhs[c]
            x_low, x_high, y_low, y_high = edges[c]
            total = along_x(fields[xx], x_low, x_high) + along_y(fields[yy], y_low, y_high) + along_z(fields[zz])
            moved = fields[c] + time_step * (buoy[...] * total)
            out[c] = moved if extra is None else moved + extra[c].reshape(size_x, size_y, size_z)

    def stress(old):
        lam_v, mu_v = lam[...], mu[...]
        vx, vy, vz = out[0], out[1], out[2]
        dxx, dyy, dzz = along_x(vx), along_y(vy), along_z(vz)
        bulk = lam_v * (dxx + dyy + dzz)
        out[3] = old[3] + time_step * (bulk + 2.0 * mu_v * dxx)
        out[4] = old[4] + time_step * (bulk + 2.0 * mu_v * dyy)
        out[5] = old[5] + time_step * (bulk + 2.0 * mu_v * dzz)
        scaled = time_step * mu_v
        out[6] = old[6] + scaled * (along_y(vx) + along_x(vy))
        out[7] = old[7] + scaled * (along_z(vx) + along_x(vz))
        out[8] = old[8] + scaled * (along_z(vy) + along_y(vz))

    def complete(turn):
        for side in range(4):
            sign = -half if side % 2 == 0 else half
            ex, ey, ez = [sign * received(turn, side)[c] for c in range(3)]
            if side < 2:
                i = 0 if side == 0 else size_x - 1
                lam_v, mu_v = lam[i], mu[i]
                bulk = lam_v * ex
                out[3, i] = out[3, i] + bulk + 2.0 * mu_v * ex
                out[4, i] = out[4, i] + bulk
                out[5, i] = out[5, i] + bulk
                out[6, i] = out[6, i] + mu_v * ey
                out[7, i] = out[7, i] + mu_v * ez
            else:
                at = pl.ds(0 if side == 2 else size_y - 1, 1)
                lam_v, mu_v = lam[:, at], mu[:, at]
                bulk = lam_v * ey
                out[3, :, at] = out[3, :, at] + bulk
                out[4, :, at] = out[4, :, at] + bulk + 2.0 * mu_v * ey
                out[5, :, at] = out[5, :, at] + bulk
                out[6, :, at] = out[6, :, at] + mu_v * ex
                out[8, :, at] = out[8, :, at] + mu_v * ez

    def stress_halo(turn):
        edges = []
        for side in range(4):
            ref = received(turn, side)
            lam_h, mu_h = received(0, side)[3], received(0, side)[4]
            sign = half if side % 2 == 0 else -half
            if side < 2:
                i = 0 if side == 0 else size_x - 1
                vx, vy, vz = [out[c, i] for c in range(3)]
                spot = lax.broadcasted_iota(jnp.int32, vx.shape, 0)
                ends = (corner_in.at[2 * side], corner_in.at[2 * side + 1])
                last = size_y - 1
            else:
                at = pl.ds(0 if side == 2 else size_y - 1, 1)
                vx, vy, vz = [out[c, :, at] for c in range(3)]
                spot = lax.broadcasted_iota(jnp.int32, vx.shape, 0)
                ends = (corner_in.at[side - 2], corner_in.at[side])
                last = size_x - 1

            def corner(c):
                return half * jnp.where(spot == 0, -ends[0][c], jnp.where(spot == last, ends[1][c], 0.0))

            stiff = sign * (lam_h + 2.0 * mu_h)
            if side < 2:
                first = ref[3] + stiff * vx + lam_h * corner(1)
                second = ref[4] + mu_h * (sign * vy + corner(0))
            else:
                first = ref[3] + mu_h * (sign * vx + corner(1))
                second = ref[4] + stiff * vy + lam_h * corner(0)
            edges.append((first, second, ref[5] + (sign * mu_h) * vz))
        return [[edges[side][c] for side in range(4)] for c in range(3)]

    def contribution():
        total = None
        for m in range(6):
            taken = sampled(out[3 + m]) * pattern[m : m + 1]
            total = taken if total is None else total + taken
        return jnp.sum(total * onehot_hi[...], axis=0, keepdims=True)

    def face(side):
        if side < 2:
            i = 0 if side == 0 else size_x - 1
            return jnp.concatenate([out[c, i] for c in range(3)], axis=0)
        at = pl.ds(0 if side == 2 else size_y - 1, 1)
        return jnp.concatenate([out[c, :, at].reshape(size_x, size_z) for c in range(3)], axis=0)

    def crossing(side):
        f = face(side)
        felt = matmul(both(f, 1), face_pick[side]) * face_weight[side, : f.shape[0]]
        return jnp.sum(felt, axis=0, keepdims=True)

    def gather_sums(step):
        pieces = jnp.concatenate([contribution()] + [crossing(side) for side in range(4)], axis=1)
        high = pieces.astype(jnp.bfloat16).astype(jnp.float32)
        mask = block_hot[...]
        stacked = jnp.concatenate([mask * high, mask * (pieces - high)], axis=0).astype(jnp.bfloat16)
        total = matmul_nt(stacked, lane_hot[...])
        sums_out[step] = (total[:blocks] + total[blocks:]).reshape(blocks, 1, LANES)

        def one(to, device):
            pltpu.make_async_remote_copy(
                src_ref=sums_out.at[step, to // per_block],
                dst_ref=sums_in.at[step, me],
                send_sem=sum_send.at[step],
                recv_sem=sum_recv.at[step],
                device_id=device,
                device_id_type=MESH,
            ).start()

        each_peer(one)
        sums_in[step, me] = sums_out[step, me // per_block]

    for side in range(4):
        pl.when(sides[side][0])(functools.partial(arrived, cross_in.at[side], cross_recv.at[side]))
    place_hi, place_lo = [place[0:1]], [place[1:2]]
    for side in range(4):
        deep = cross_in[side, 4:5].astype(jnp.int32)
        chosen_deep = one_hot((size_z, entries), 0, deep)
        face_pick[side] = jnp.concatenate([chosen_deep, chosen_deep], axis=0)
        span = size_y if side < 2 else size_x
        on_row = lax.broadcasted_iota(jnp.int32, (span, entries), 0) == cross_in[side, 3:4].astype(jnp.int32)
        for c in range(3):
            face_weight[side, c * span : (c + 1) * span] = jnp.where(on_row, cross_in[side, c : c + 1], 0.0)
        place_hi.append(cross_in[side, 5:6])
        place_lo.append(cross_in[side, 6:7])
    place_hi = jnp.concatenate(place_hi, axis=1).astype(jnp.int32)
    place_lo = jnp.concatenate(place_lo, axis=1).astype(jnp.int32)
    block_hot[...] = jnp.where(lax.broadcasted_iota(jnp.int32, block_hot.shape, 0) == place_hi, 1.0, 0.0)
    lane_hot[...] = one_hot(lane_hot.shape, 0, place_lo)

    receive(0)
    velocity(state, [halo(0, c) for c in range(3)], None)

    from_peers = landed.at[pl.ds(0, count - 1)]
    arrived(from_peers, route_recv)
    lane = lax.broadcasted_iota(jnp.int32, (8, LANES), 1) // slot_count
    boxes = []
    for v in range(8):
        flat = []
        for base in range(0, count, 8 * group):
            total = jnp.zeros((8, LANES), jnp.float32)
            for j in range(group):
                piece = landed[base + 8 * j : base + 8 * j + 8, v // group, :]
                turn = ((j - v % group) * slot_count) % LANES
                total = jnp.where(lane == j, pltpu.roll(piece, turn, 1) if turn else piece, total)
            flat.extend(total[i : i + 1] for i in range(8))
        boxes.append(jnp.concatenate(flat, axis=1))
    inbox = jnp.concatenate(boxes, axis=0)
    spread_lo = one_hot((size_z, slots), 0, inbox[7:8].astype(jnp.int32))
    spread_lo = jnp.concatenate([spread_lo, spread_lo], axis=1)
    row_mask = lax.broadcasted_iota(jnp.int32, (rows, slots), 0) == inbox[6:7].astype(jnp.int32)
    amp_hi, amp_lo = split(inbox)
    amp_hi, amp_lo = amp_hi.astype(jnp.float32), amp_lo.astype(jnp.float32)

    def injected(m):
        high = jnp.where(row_mask, amp_hi[m : m + 1], 0.0).astype(jnp.bfloat16)
        low = jnp.where(row_mask, amp_lo[m : m + 1], 0.0).astype(jnp.bfloat16)
        return matmul_nt(jnp.concatenate([high, low], axis=1), spread_lo)

    for c in range(3):
        out[c] = out[c] + injected(c).reshape(size_x, size_y, size_z)

    for step in range(steps):
        last = step == steps - 1
        if step:
            receive(step)
            complete(step)
            for q in range(4):
                pl.when(corners[q][0])(functools.partial(arrived, corner_in.at[q], corner_recv.at[q]))
            velocity(out, stress_halo(step), [source[(step - 1) * 3 + c] for c in range(3)])
        stress(out if step else state)
        if last:
            gather_sums(step)
        flow = [out[c] for c in range(3)]
        stage(step + 1, 0, flow, flow)
        if not last:
            stage(step + 1, 3, [out[i] for i in stress_x], [out[i] for i in stress_y])
            for q in range(4):
                i, j = (0, size_x - 1)[q // 2], (0, size_y - 1)[q % 2]
                for c in range(2):
                    corner_out[q, c] = out[c, i, j : j + 1]
            send(corner_copies(), corners)
        send(halo_copies(step + 1), sides)
        if not last:
            for m in range(3):
                source[step * 3 + m] = injected((step + 1) * 3 + m)
            gather_sums(step)
    receive(steps)
    complete(steps)

    first = lax.rem(me, per_block) * owned
    for step in range(steps):
        all_sums = sums_in.at[step, pl.ds(0, count - 1)]
        arrived(all_sums, sum_recv.at[step])
        final = jnp.sum(sums_in[step], axis=0)
        final = jnp.concatenate([final, jnp.zeros((7, LANES), jnp.float32)], axis=0)
        slip[step : step + 1] = pltpu.roll(final, lax.rem(LANES - first, LANES), 1)[:1, :owned]

    arrived(from_peers, route_send)
    for step in range(steps):
        arrived(sums_in.at[step, pl.ds(0, count - 1)], sum_send.at[step])
    for turn in range(turns):
        for side, copy in enumerate(halo_copies(turn)):
            pl.when(sides[side][0])(copy.wait_send)
    for side, copy in enumerate(cross_copies()):
        pl.when(sides[side][0])(copy.wait_send)
    for q, copy in enumerate(corner_copies()):
        pl.when(corners[q][0])(copy.wait_send)


def put(state, slip, out, grad, sems):
    copies = [pltpu.make_async_copy(state, out, sems.at[0]), pltpu.make_async_copy(slip, grad, sems.at[1])]
    for copy in copies:
        copy.start()
    for copy in copies:
        copy.wait()


def shards(
    adjoint_state,
    lame_lambda,
    lame_mu,
    buoyancy,
    residual,
    receiver_tile,
    receiver_cell,
    resample,
    fault_patch,
    fault_cell,
    fault_area,
    moment,
    subpatch_order,
):
    strike_count = lax.axis_size("strike")
    dip_count = lax.axis_size("dip")
    count = strike_count * dip_count
    stations = residual.shape[0]
    slot_count = max(2, (2 * stations + count - 1) // count)
    steps = resample.shape[0]
    size_x, size_y, size_z = buoyancy.shape
    rows = size_x * size_y
    group = LANES // slot_count
    value_rows = -(-8 // group)
    assert count % (8 * group) == 0 and group * slot_count == LANES
    entries = fault_patch.shape[1]
    patches = moment.shape[1]
    blocks = patches // LANES
    assert steps * 3 + 2 == 8
    anywhere = pl.BlockSpec(memory_space=pl.ANY)
    vmem = pl.BlockSpec(memory_space=pltpu.VMEM)
    f32, bf16 = jnp.float32, jnp.bfloat16
    operands = (
        adjoint_state,
        lame_lambda,
        lame_mu,
        buoyancy,
        jnp.swapaxes(residual, 0, 1),
        receiver_tile.reshape(1, stations),
        receiver_cell.reshape(1, stations),
        resample,
        fault_patch,
        fault_cell,
        fault_area,
        moment,
        subpatch_order.reshape(1, -1),
    )
    halves = []
    for fields in [5] + [6] * (steps - 1) + [3]:
        along, across = (fields, size_y, size_z), (fields, size_x, 1, size_z)
        halves += [pltpu.VMEM(shape, f32) for shape in ((2, *along), along, along, (2, *across), across, across)]
    state, slip = pl.pallas_call(
        functools.partial(kernel, strike_count, dip_count, slot_count),
        out_shape=(
            pltpu.VMEM(adjoint_state.shape, f32),
            pltpu.VMEM((steps, patches // count), f32),
        ),
        in_specs=[anywhere] * 13,
        out_specs=(vmem, vmem),
        scratch_shapes=[
            *(pltpu.VMEM(a.shape, a.dtype) for a in operands),
            *halves,
            pltpu.VMEM((count, value_rows, LANES), f32),
            pltpu.VMEM((count, value_rows, LANES), f32),
            pltpu.VMEM((steps * 3 - 3, rows, size_z), f32),
            pltpu.VMEM((rows, entries), f32),
            pltpu.VMEM((2 * size_z, entries), bf16),
            pltpu.VMEM((4, 2 * size_z, entries), bf16),
            pltpu.VMEM((4, 3 * max(size_x, size_y), entries), f32),
            pltpu.VMEM((blocks, 5 * entries), f32),
            pltpu.VMEM((LANES, 5 * entries), bf16),
            pltpu.VMEM((4, 2, 1, size_z), f32),
            pltpu.VMEM((4, 2, 1, size_z), f32),
            pltpu.VMEM((4, 8, entries), f32),
            pltpu.VMEM((4, 8, entries), f32),
            pltpu.VMEM((steps, blocks, 1, LANES), f32),
            pltpu.VMEM((steps, count, 1, LANES), f32),
            pltpu.SemaphoreType.DMA((13,)),
            pltpu.SemaphoreType.DMA,
            pltpu.SemaphoreType.DMA,
            pltpu.SemaphoreType.DMA((steps + 1, 4)),
            pltpu.SemaphoreType.DMA((steps + 1, 4)),
            pltpu.SemaphoreType.DMA((4,)),
            pltpu.SemaphoreType.DMA((4,)),
            pltpu.SemaphoreType.DMA((4,)),
            pltpu.SemaphoreType.DMA((4,)),
            pltpu.SemaphoreType.DMA((steps,)),
            pltpu.SemaphoreType.DMA((steps,)),
        ],
        compiler_params=pltpu.CompilerParams(collective_id=0, has_side_effects=True),
        name="adjoint",
    )(*operands)
    state = pltpu.with_memory_space_constraint(state, pltpu.VMEM)
    slip = pltpu.with_memory_space_constraint(slip, pltpu.VMEM)
    return pl.pallas_call(
        put,
        out_shape=(
            jax.ShapeDtypeStruct(state.shape, f32),
            jax.ShapeDtypeStruct(slip.shape, f32),
        ),
        in_specs=[vmem, vmem],
        out_specs=(anywhere, anywhere),
        scratch_shapes=[pltpu.SemaphoreType.DMA((2,))],
        name="put",
    )(state, slip)


def solution(mesh):
    return jax.shard_map(
        shards,
        mesh=mesh,
        in_specs=(
            P(None, "strike", "dip", None),
            P("strike", "dip", None),
            P("strike", "dip", None),
            P("strike", "dip", None),
            P(("strike", "dip"), None, None),
            P(("strike", "dip"), None),
            P(("strike", "dip")),
            P(),
            P(("strike", "dip"), None),
            P(("strike", "dip"), None),
            P(("strike", "dip"), None),
            P(),
            P(),
        ),
        out_specs=(P(None, "strike", "dip", None), P(None, ("strike", "dip"))),
        check_vma=False,
    )
```

```python
import functools

import jax
import jax.numpy as jnp
from jax import lax
from jax.experimental import pallas as pl
from jax.experimental.pallas import tpu as pltpu
from jax.sharding import PartitionSpec as P

LANES = 128

time_step = 0.25

MESH = pl.DeviceIdType.MESH
NT_DIMS = (((1,), (1,)), ((), ()))


def split(x):
    high = x.astype(jnp.bfloat16)
    return high, (x - high.astype(jnp.float32)).astype(jnp.bfloat16)


def one_hot(shape, axis, ids):
    return jnp.where(lax.broadcasted_iota(jnp.int32, shape, axis) == ids, 1.0, 0.0).astype(jnp.bfloat16)


def matmul(a, b):
    return jnp.dot(a, b, preferred_element_type=jnp.float32)


def matmul_nt(a, b):
    return lax.dot_general(a, b, NT_DIMS, preferred_element_type=jnp.float32)


def along_x(f, low=None, high=None):
    low = jnp.zeros_like(f[0]) if low is None else low
    high = jnp.zeros_like(f[0]) if high is None else high
    before = jnp.concatenate([low[None], f[:-1]], axis=0)
    after = jnp.concatenate([f[1:], high[None]], axis=0)
    return (after - before) * 0.5


def along_y(f, low=0.0, high=0.0):
    size = f.shape[1]
    at = lax.broadcasted_iota(jnp.int32, f.shape, 1)
    before = jnp.where(at == 0, low, pltpu.roll(f, 1, 1))
    after = jnp.where(at == size - 1, high, pltpu.roll(f, size - 1, 1))
    return (after - before) * 0.5


def along_z(f):
    size = f.shape[2]
    at = lax.broadcasted_iota(jnp.int32, f.shape, 2)
    before = jnp.where(at == 0, 0.0, pltpu.roll(f, 1, 2))
    after = jnp.where(at == size - 1, 0.0, pltpu.roll(f, size - 1, 2))
    return (after - before) * 0.5


def both(x, axis):
    return jnp.concatenate(split(x), axis=axis)


def kernel(strike_count, dip_count, slot_count, *refs):
    far, refs = refs[:13], refs[13:]
    (out, slip), refs = refs[:2], refs[2:]
    near, refs = refs[:13], refs[13:]
    state, lam, mu, buoy, residual, tiles, cells, resample, patch, fault_cell, area, moment, order = near
    steps = resample.shape[0]
    turns = 2 * steps
    halves, refs = [refs[6 * t : 6 * t + 6] for t in range(turns)], refs[6 * turns :]
    (
        packed,
        landed,
        source,
        onehot_hi,
        pick,
        slope,
        face_pick,
        face_weight,
        block_hot,
        lane_hot,
        corner_out,
        corner_in,
        cross_out,
        cross_in,
        sums_out,
        sums_in,
        fetch_sem,
        route_send,
        route_recv,
        halo_send,
        halo_recv,
        corner_send,
        corner_recv,
        cross_send,
        cross_recv,
        sum_send,
        sum_recv,
    ) = refs
    count = strike_count * dip_count
    strike = lax.axis_index("strike")
    dip = lax.axis_index("dip")
    me = strike * dip_count + dip
    size_x, size_y, size_z = buoy.shape
    rows = size_x * size_y
    stations = residual.shape[1]
    entries = patch.shape[1]
    shift = size_z.bit_length() - 1
    group = LANES // slot_count
    value_rows = packed.shape[1]
    owned = order.shape[1] // count
    per_block = LANES // owned
    blocks = order.shape[1] // LANES
    half = 0.5 * time_step
    near_count = count // 2
    near_half = 2 * dip // dip_count
    here = dip * strike_count + strike
    halves_at = (near_half * near_count, (1 - near_half) * near_count)
    slots = near_count * slot_count

    flip_strike = strike < strike_count // 2
    flip_dip = dip < dip_count // 2

    def turned(flip, size, k):
        return jnp.where(flip, size - 1 - k, k)

    skip = turned(flip_dip, dip_count, dip) * strike_count + turned(flip_strike, strike_count, strike)

    def each_peer(act):
        def one(n, carry):
            at = n + jnp.where(n >= skip, 1, 0)
            to_strike = turned(flip_strike, strike_count, lax.rem(at, strike_count))
            to_dip = turned(flip_dip, dip_count, at // strike_count)
            act(to_strike * dip_count + to_dip, (to_strike, to_dip))
            return carry

        lax.fori_loop(0, count - 1, one, 0)

    barrier = pltpu.get_barrier_semaphore()
    fetches = [pltpu.make_async_copy(far[i], near[i], fetch_sem.at[i]) for i in range(13)]
    early = (5, 6, 7, 4)
    each_peer(lambda to, device: pl.semaphore_signal(barrier, inc=1, device_id=device, device_id_type=MESH))

    for i in early:
        fetches[i].start()
    for i in range(13):
        if i not in early:
            fetches[i].start()

    sides = (
        (strike > 0, (strike - 1, dip)),
        (strike < strike_count - 1, (strike + 1, dip)),
        (dip > 0, (strike, dip - 1)),
        (dip < dip_count - 1, (strike, dip + 1)),
    )
    corners = tuple(
        (jnp.logical_and(sides[a][0], sides[2 + b][0]), (strike + 2 * a - 1, dip + 2 * b - 1))
        for a in range(2)
        for b in range(2)
    )

    def halo_copies(turn):
        x_out, x_low, x_high, y_out, y_low, y_high = halves[turn]
        copies = []
        for side in range(4):
            sender, low, high = (x_out, x_low, x_high) if side < 2 else (y_out, y_low, y_high)
            copies.append(
                pltpu.make_async_remote_copy(
                    src_ref=sender.at[side % 2],
                    dst_ref=high if side % 2 == 0 else low,
                    send_sem=halo_send.at[turn, side],
                    recv_sem=halo_recv.at[turn, side ^ 1],
                    device_id=sides[side][1],
                    device_id_type=MESH,
                )
            )
        return copies

    def corner_copies():
        return [
            pltpu.make_async_remote_copy(
                src_ref=corner_out.at[q],
                dst_ref=corner_in.at[3 - q],
                send_sem=corner_send.at[q],
                recv_sem=corner_recv.at[3 - q],
                device_id=corners[q][1],
                device_id_type=MESH,
            )
            for q in range(4)
        ]

    def cross_copies():
        return [
            pltpu.make_async_remote_copy(
                src_ref=cross_out.at[side],
                dst_ref=cross_in.at[side ^ 1],
                send_sem=cross_send.at[side],
                recv_sem=cross_recv.at[side ^ 1],
                device_id=sides[side][1],
                device_id_type=MESH,
            )
            for side in range(4)
        ]

    def received(turn, side):
        return halves[turn][(1, 2, 4, 5)[side]]

    def arrived(ref, sem):
        pltpu.make_async_copy(ref, ref, sem).wait()

    def stage(turn, at, x_face, y_face):
        x_out, y_out = halves[turn][0], halves[turn][3]
        for c in range(len(x_face)):
            f = x_face[c]
            x_out[0, at + c] = f[0]
            x_out[1, at + c] = f[size_x - 1]
            f = y_face[c]
            y_out[0, at + c] = f[:, 0:1]
            y_out[1, at + c] = f[:, size_y - 1 : size_y]

    def send(copies, where):
        for side, copy in enumerate(copies):
            pl.when(where[side][0])(copy.start)

    def receive(turn):
        for side in range(4):
            pl.when(sides[side][0])(functools.partial(arrived, received(turn, side), halo_recv.at[turn, side]))

    earlier = jnp.where(
        lax.broadcasted_iota(jnp.int32, (stations, stations), 0) < lax.broadcasted_iota(jnp.int32, (stations, stations), 1),
        1.0,
        0.0,
    ).astype(jnp.bfloat16)

    stress_x, stress_y = (3, 6, 7), (6, 4, 8)
    for i in early:
        fetches[i].wait()

    weights = both(resample[...] * time_step, 0)
    parts = [matmul_nt(weights, residual[c]) for c in range(3)]
    amplitude = [parts[c][k : k + 1] + parts[c][steps + k : steps + k + 1] for k in range(steps) for c in range(3)]
    cell_row = cells[...]
    hi_row = lax.shift_right_logical(cell_row, shift).astype(jnp.float32)
    lo_row = (cell_row & (size_z - 1)).astype(jnp.float32)
    values = jnp.concatenate(amplitude + [hi_row, lo_row], axis=0)
    named = one_hot((count, stations), 0, tiles[...])
    ordinal = jnp.sum(named.astype(jnp.float32) * matmul(named, earlier), axis=0, keepdims=True)
    slot_hot = lax.broadcasted_iota(jnp.int32, (slot_count, stations), 0) == ordinal.astype(jnp.int32)
    spread = []
    for r in range(value_rows):
        for part in split(values):
            pieces = [
                jnp.where(slot_hot, part[v : v + 1].astype(jnp.float32), 0.0)
                for v in range(r * group, min(8, (r + 1) * group))
            ]
            used = len(pieces) * slot_count
            if used < LANES:
                pieces.append(jnp.zeros((LANES - used, stations), jnp.float32))
            spread.append(jnp.concatenate(pieces, axis=0).astype(jnp.bfloat16))
    placed = matmul_nt(named, jnp.concatenate(spread, axis=0))
    for r in range(value_rows):
        at = 2 * r * LANES
        packed[:, r, :] = placed[:, at : at + LANES] + placed[:, at + LANES : at + 2 * LANES]

    pl.semaphore_wait(barrier, count - 1)

    def route(to, device):
        pltpu.make_async_remote_copy(
            src_ref=packed.at[to],
            dst_ref=landed.at[here],
            send_sem=route_send,
            recv_sem=route_recv.at[jnp.where(2 * device[1] // dip_count == near_half, 0, 1)],
            device_id=device,
            device_id_type=MESH,
        ).start()

    each_peer(route)
    landed[here] = packed[me]
    for i in (0, 1, 2):
        fetches[i].wait()
    stage(0, 0, [state[i] for i in stress_x], [state[i] for i in stress_y])
    stage(0, 3, [lam[...], mu[...]], [lam[...], mu[...]])
    send(halo_copies(0), sides)
    for i in range(3, 13):
        if i not in early:
            fetches[i].wait()

    for side in range(4):

        def clear(side=side):
            for turn in range(turns):
                target = received(turn, side)
                target[...] = jnp.zeros_like(target)
            cross_in[side] = jnp.zeros_like(cross_in[side])

        pl.when(jnp.logical_not(sides[side][0]))(clear)
    for q in range(4):

        def clear_corner(q=q):
            corner_in[q] = jnp.zeros_like(corner_in[q])

        pl.when(jnp.logical_not(corners[q][0]))(clear_corner)

    patch_row = patch[...]
    cell_e = fault_cell[...]
    row_e = lax.shift_right_logical(cell_e, shift)
    deep_e = cell_e & (size_z - 1)
    pick_lo = one_hot((size_z, entries), 0, deep_e)
    deep_iota = lax.broadcasted_iota(jnp.int32, (size_z, entries), 0)
    pick_slope = jnp.where(deep_iota == deep_e + 1, 1.0, jnp.where(deep_iota == deep_e - 1, -1.0, 0.0)).astype(jnp.bfloat16)
    pick_both = jnp.concatenate([pick_lo, pick_slope], axis=1)
    pick[...] = jnp.concatenate([pick_both, pick_both], axis=0)
    offset = lax.broadcasted_iota(jnp.int32, (rows, entries), 0) - row_e
    onehot_hi[...] = jnp.where(offset == 0, 1.0, 0.0)
    chosen = matmul(both(moment[...], 0), one_hot((moment.shape[1], entries), 0, patch_row))
    pattern = (chosen[:6] + chosen[6:]) * area[...]
    patch_col = jnp.transpose(jnp.broadcast_to(patch_row.astype(jnp.float32), (LANES, entries)))
    picks = jnp.concatenate(
        [
            jnp.where(patch_col == order[:, b * LANES : (b + 1) * LANES].astype(jnp.float32), 1.0, 0.0).astype(
                jnp.bfloat16
            )
            for b in range(blocks)
        ],
        axis=1,
    )
    number = lax.broadcasted_iota(jnp.int32, (8, order.shape[1]), 1)
    which = lax.broadcasted_iota(jnp.int32, (8, order.shape[1]), 0)
    number = jnp.where(which == 0, number // LANES, number % LANES).astype(jnp.float32).astype(jnp.bfloat16)
    place = matmul_nt(number, picks)[:2]

    def sampled(field):
        return matmul(both(field.reshape(rows, size_z), 1), pick[:, :entries])

    def at_entries(field):
        return jnp.sum(sampled(field) * onehot_hi[...], axis=0, keepdims=True)

    lam_e, mu_e = at_entries(lam[...]), at_entries(mu[...])
    stiff_e = lam_e + 2.0 * mu_e
    pxx, pyy, pzz, pxy, pxz, pyz = [pattern[m : m + 1] for m in range(6)]
    x_e, y_e = row_e // size_y, lax.rem(row_e, size_y)
    x_weight = (pxx * stiff_e + (pyy + pzz) * lam_e, pxy * mu_e, pxz * mu_e)
    y_weight = (pxy * mu_e, pyy * stiff_e + (pxx + pzz) * lam_e, pyz * mu_e)
    z_weight = (pxz * mu_e, pyz * mu_e, pzz * stiff_e + (pxx + pyy) * lam_e)
    for c in range(3):
        along, across, upward = half * x_weight[c], half * y_weight[c], half * z_weight[c]
        above = jnp.where(y_e < size_y - 1, across, 0.0)
        below = jnp.where(y_e > 0, -across, 0.0)
        grown = jnp.where(offset == size_y, along, jnp.where(offset == -size_y, -along, 0.0))
        slope[c, :, :entries] = jnp.where(offset == 1, above, jnp.where(offset == -1, below, grown))
        slope[c, :, entries:] = jnp.where(offset == 0, upward, 0.0)
    tail = [deep_e.astype(jnp.float32), place, jnp.zeros((1, entries), jnp.float32)]
    for side in range(4):
        on, across, weight = (x_e, y_e, x_weight) if side < 2 else (y_e, x_e, y_weight)
        edge = 0 if side % 2 == 0 else (size_x if side < 2 else size_y) - 1
        scale = jnp.where(on == edge, -half if side % 2 == 0 else half, 0.0)
        cross_out[side] = jnp.concatenate([w * scale for w in weight] + [across.astype(jnp.float32)] + tail, axis=0)
    send(cross_copies(), sides)

    def halo(turn, c):
        return [received(turn, side)[c] for side in range(4)]

    rhs = ((3, 6, 7), (6, 4, 8), (7, 8, 5))

    def velocity(fields, edges, extra):
        for c in range(3):
            xx, yy, zz = rhs[c]
            x_low, x_high, y_low, y_high = edges[c]
            total = along_x(fields[xx], x_low, x_high) + along_y(fields[yy], y_low, y_high) + along_z(fields[zz])
            moved = fields[c] + time_step * (buoy[...] * total)
            out[c] = moved if extra is None else moved + extra[c].reshape(size_x, size_y, size_z)

    def stress(old):
        lam_v, mu_v = lam[...], mu[...]
        vx, vy, vz = out[0], out[1], out[2]
        dxx, dyy, dzz = along_x(vx), along_y(vy), along_z(vz)
        bulk = lam_v * (dxx + dyy + dzz)
        out[3] = old[3] + time_step * (bulk + 2.0 * mu_v * dxx)
        out[4] = old[4] + time_step * (bulk + 2.0 * mu_v * dyy)
        out[5] = old[5] + time_step * (bulk + 2.0 * mu_v * dzz)
        scaled = time_step * mu_v
        out[6] = old[6] + scaled * (along_y(vx) + along_x(vy))
        out[7] = old[7] + scaled * (along_z(vx) + along_x(vz))
        out[8] = old[8] + scaled * (along_z(vy) + along_y(vz))

    def complete(turn):
        for side in range(4):
            sign = -half if side % 2 == 0 else half
            ex, ey, ez = [sign * received(turn, side)[c] for c in range(3)]
            if side < 2:
                i = 0 if side == 0 else size_x - 1
                lam_v, mu_v = lam[i], mu[i]
                bulk = lam_v * ex
                out[3, i] = out[3, i] + bulk + 2.0 * mu_v * ex
                out[4, i] = out[4, i] + bulk
                out[5, i] = out[5, i] + bulk
                out[6, i] = out[6, i] + mu_v * ey
                out[7, i] = out[7, i] + mu_v * ez
            else:
                at = pl.ds(0 if side == 2 else size_y - 1, 1)
                lam_v, mu_v = lam[:, at], mu[:, at]
                bulk = lam_v * ey
                out[3, :, at] = out[3, :, at] + bulk
                out[4, :, at] = out[4, :, at] + bulk + 2.0 * mu_v * ey
                out[5, :, at] = out[5, :, at] + bulk
                out[6, :, at] = out[6, :, at] + mu_v * ex
                out[8, :, at] = out[8, :, at] + mu_v * ez

    def stress_halo(turn):
        edges = []
        for side in range(4):
            ref = received(turn, side)
            lam_h, mu_h = received(0, side)[3], received(0, side)[4]
            sign = half if side % 2 == 0 else -half
            if side < 2:
                i = 0 if side == 0 else size_x - 1
                vx, vy, vz = [out[c, i] for c in range(3)]
                spot = lax.broadcasted_iota(jnp.int32, vx.shape, 0)
                ends = (corner_in.at[2 * side], corner_in.at[2 * side + 1])
                last = size_y - 1
            else:
                at = pl.ds(0 if side == 2 else size_y - 1, 1)
                vx, vy, vz = [out[c, :, at] for c in range(3)]
                spot = lax.broadcasted_iota(jnp.int32, vx.shape, 0)
                ends = (corner_in.at[side - 2], corner_in.at[side])
                last = size_x - 1

            def corner(c):
                return half * jnp.where(spot == 0, -ends[0][c], jnp.where(spot == last, ends[1][c], 0.0))

            stiff = sign * (lam_h + 2.0 * mu_h)
            if side < 2:
                first = ref[0] + stiff * vx + lam_h * corner(1)
                second = ref[1] + mu_h * (sign * vy + corner(0))
            else:
                first = ref[0] + mu_h * (sign * vx + corner(1))
                second = ref[1] + stiff * vy + lam_h * corner(0)
            edges.append((first, second, ref[2] + (sign * mu_h) * vz))
        return [[edges[side][c] for side in range(4)] for c in range(3)]

    def initial():
        total = None
        for m in range(6):
            taken = sampled(state[3 + m]) * pattern[m : m + 1]
            total = taken if total is None else total + taken
        return jnp.sum(total * onehot_hi[...], axis=0, keepdims=True)

    start_e = initial()

    def contribution():
        total = None
        for c in range(3):
            taken = matmul(both(out[c].reshape(rows, size_z), 1), pick[...]) * slope[c]
            taken = taken[:, :entries] + taken[:, entries:]
            total = taken if total is None else total + taken
        return jnp.sum(total, axis=0, keepdims=True)

    def face(side):
        if side < 2:
            i = 0 if side == 0 else size_x - 1
            return jnp.concatenate([out[c, i] for c in range(3)], axis=0)
        at = pl.ds(0 if side == 2 else size_y - 1, 1)
        return jnp.concatenate([out[c, :, at].reshape(size_x, size_z) for c in range(3)], axis=0)

    def crossing(side):
        f = face(side)
        felt = matmul(both(f, 1), face_pick[side]) * face_weight[side, : f.shape[0]]
        return jnp.sum(felt, axis=0, keepdims=True)

    def gather_sums(step, before):
        own = contribution()
        own = own if step else own + start_e
        pieces = jnp.concatenate([own] + [crossing(side) for side in range(4)], axis=1)
        high = pieces.astype(jnp.bfloat16).astype(jnp.float32)
        mask = block_hot[...]
        stacked = jnp.concatenate([mask * high, mask * (pieces - high)], axis=0).astype(jnp.bfloat16)
        total = matmul_nt(stacked, lane_hot[...])
        total = total[:blocks] + total[blocks:]
        total = total if before is None else before + total
        sums_out[step] = total.reshape(blocks, 1, LANES)

        def one(to, device):
            pltpu.make_async_remote_copy(
                src_ref=sums_out.at[step, to // per_block],
                dst_ref=sums_in.at[step, me],
                send_sem=sum_send.at[step],
                recv_sem=sum_recv.at[step],
                device_id=device,
                device_id_type=MESH,
            ).start()

        each_peer(one)
        sums_in[step, me] = sums_out[step, me // per_block]
        return total

    def meet():
        for side in range(4):
            pl.when(sides[side][0])(functools.partial(arrived, cross_in.at[side], cross_recv.at[side]))
        place_hi, place_lo = [place[0:1]], [place[1:2]]
        for side in range(4):
            deep = cross_in[side, 4:5].astype(jnp.int32)
            chosen_deep = one_hot((size_z, entries), 0, deep)
            face_pick[side] = jnp.concatenate([chosen_deep, chosen_deep], axis=0)
            span = size_y if side < 2 else size_x
            on_row = lax.broadcasted_iota(jnp.int32, (span, entries), 0) == cross_in[side, 3:4].astype(jnp.int32)
            for c in range(3):
                face_weight[side, c * span : (c + 1) * span] = jnp.where(on_row, cross_in[side, c : c + 1], 0.0)
            place_hi.append(cross_in[side, 5:6])
            place_lo.append(cross_in[side, 6:7])
        place_hi = jnp.concatenate(place_hi, axis=1).astype(jnp.int32)
        place_lo = jnp.concatenate(place_lo, axis=1).astype(jnp.int32)
        block_hot[...] = jnp.where(lax.broadcasted_iota(jnp.int32, block_hot.shape, 0) == place_hi, 1.0, 0.0)
        lane_hot[...] = one_hot(lane_hot.shape, 0, place_lo)

    lane = lax.broadcasted_iota(jnp.int32, (slots // LANES, LANES), 1) // slot_count

    def unpacked(start):
        boxes = []
        high = slots // LANES
        for v in range(8):
            total = jnp.zeros((high, LANES), jnp.float32)
            for j in range(group):
                piece = landed[pl.ds(start + high * j, high), v // group, :]
                turn = ((j - v % group) * slot_count) % LANES
                total = jnp.where(lane == j, pltpu.roll(piece, turn, 1) if turn else piece, total)
            boxes.append(jnp.concatenate([total[i : i + 1] for i in range(high)], axis=1))
        inbox = jnp.concatenate(boxes, axis=0)
        spread_lo = one_hot((size_z, slots), 0, inbox[7:8].astype(jnp.int32))
        spread_lo = jnp.concatenate([spread_lo, spread_lo], axis=1)
        row_mask = lax.broadcasted_iota(jnp.int32, (rows, slots), 0) == inbox[6:7].astype(jnp.int32)
        amp_hi, amp_lo = split(inbox)
        return row_mask, spread_lo, amp_hi.astype(jnp.float32), amp_lo.astype(jnp.float32)

    def injected(box, m):
        row_mask, spread_lo, amp_hi, amp_lo = box
        high = jnp.where(row_mask, amp_hi[m : m + 1], 0.0).astype(jnp.bfloat16)
        low = jnp.where(row_mask, amp_lo[m : m + 1], 0.0).astype(jnp.bfloat16)
        return matmul_nt(jnp.concatenate([high, low], axis=1), spread_lo)

    arrived(landed.at[pl.ds(0, near_count - 1)], route_recv.at[0])
    box_near = unpacked(halves_at[0])
    first = [injected(box_near, c) for c in range(3)]
    receive(0)
    velocity(state, [halo(0, c) for c in range(3)], first)
    arrived(landed.at[pl.ds(0, near_count)], route_recv.at[1])
    box_far = unpacked(halves_at[1])
    for c in range(3):
        out[c] = out[c] + injected(box_far, c).reshape(size_x, size_y, size_z)

    total = None
    for step in range(steps):
        last = step == steps - 1
        turn = 2 * step + 1
        if step:
            receive(turn - 2)
            complete(turn - 2)
            receive(turn - 1)
            for q in range(4):
                pl.when(corners[q][0])(functools.partial(arrived, corner_in.at[q], corner_recv.at[q]))
            velocity(out, stress_halo(turn - 1), [source[(step - 1) * 3 + c] for c in range(3)])
        flow = [out[c] for c in range(3)]
        if last:
            total = gather_sums(step, total)
        else:
            for q in range(4):
                i, j = (0, size_x - 1)[q // 2], (0, size_y - 1)[q % 2]
                for c in range(2):
                    corner_out[q, c] = out[c, i, j : j + 1]
            send(corner_copies(), corners)
        stage(turn, 0, flow, flow)
        send(halo_copies(turn), sides)
        stress(out if step else state)
        if not last:
            stage(turn + 1, 0, [out[i] for i in stress_x], [out[i] for i in stress_y])
            send(halo_copies(turn + 1), sides)
            if step == 0:
                meet()
            for m in range(3):
                at = (step + 1) * 3 + m
                source[at - 3] = injected(box_near, at) + injected(box_far, at)
            total = gather_sums(step, total)
    receive(turns - 1)
    complete(turns - 1)

    first = lax.rem(me, per_block) * owned
    for step in range(steps):
        all_sums = sums_in.at[step, pl.ds(0, count - 1)]
        arrived(all_sums, sum_recv.at[step])
        final = jnp.sum(sums_in[step], axis=0)
        final = jnp.concatenate([final, jnp.zeros((7, LANES), jnp.float32)], axis=0)
        slip[step : step + 1] = pltpu.roll(final, lax.rem(LANES - first, LANES), 1)[:1, :owned]

    arrived(landed.at[pl.ds(0, count - 1)], route_send)
    for step in range(steps):
        arrived(sums_in.at[step, pl.ds(0, count - 1)], sum_send.at[step])
    for turn in range(turns):
        for side, copy in enumerate(halo_copies(turn)):
            pl.when(sides[side][0])(copy.wait_send)
    for side, copy in enumerate(cross_copies()):
        pl.when(sides[side][0])(copy.wait_send)
    for q, copy in enumerate(corner_copies()):
        pl.when(corners[q][0])(copy.wait_send)


def put(state, slip, out, grad, sems):
    copies = [pltpu.make_async_copy(state, out, sems.at[0]), pltpu.make_async_copy(slip, grad, sems.at[1])]
    for copy in copies:
        copy.start()
    for copy in copies:
        copy.wait()


def shards(
    adjoint_state,
    lame_lambda,
    lame_mu,
    buoyancy,
    residual,
    receiver_tile,
    receiver_cell,
    resample,
    fault_patch,
    fault_cell,
    fault_area,
    moment,
    subpatch_order,
):
    strike_count = lax.axis_size("strike")
    dip_count = lax.axis_size("dip")
    count = strike_count * dip_count
    stations = residual.shape[0]
    slot_count = max(2, (2 * stations + count - 1) // count)
    steps = resample.shape[0]
    size_x, size_y, size_z = buoyancy.shape
    rows = size_x * size_y
    group = LANES // slot_count
    value_rows = -(-8 // group)
    assert dip_count % 2 == 0 and count * slot_count % (2 * LANES) == 0 and group * slot_count == LANES
    entries = fault_patch.shape[1]
    patches = moment.shape[1]
    blocks = patches // LANES
    assert steps * 3 + 2 == 8
    anywhere = pl.BlockSpec(memory_space=pl.ANY)
    vmem = pl.BlockSpec(memory_space=pltpu.VMEM)
    f32, bf16 = jnp.float32, jnp.bfloat16
    operands = (
        adjoint_state,
        lame_lambda,
        lame_mu,
        buoyancy,
        jnp.swapaxes(residual, 0, 1),
        receiver_tile.reshape(1, stations),
        receiver_cell.reshape(1, stations),
        resample,
        fault_patch,
        fault_cell,
        fault_area,
        moment,
        subpatch_order.reshape(1, -1),
    )
    halves = []
    for fields in [5] + [3] * (2 * steps - 1):
        along, across = (fields, size_y, size_z), (fields, size_x, 1, size_z)
        halves += [pltpu.VMEM(shape, f32) for shape in ((2, *along), along, along, (2, *across), across, across)]
    state, slip = pl.pallas_call(
        functools.partial(kernel, strike_count, dip_count, slot_count),
        out_shape=(
            pltpu.VMEM(adjoint_state.shape, f32),
            pltpu.VMEM((steps, patches // count), f32),
        ),
        in_specs=[anywhere] * 13,
        out_specs=(vmem, vmem),
        scratch_shapes=[
            *(pltpu.VMEM(a.shape, a.dtype) for a in operands),
            *halves,
            pltpu.VMEM((count, value_rows, LANES), f32),
            pltpu.VMEM((count, value_rows, LANES), f32),
            pltpu.VMEM((steps * 3 - 3, rows, size_z), f32),
            pltpu.VMEM((rows, entries), f32),
            pltpu.VMEM((2 * size_z, 2 * entries), bf16),
            pltpu.VMEM((3, rows, 2 * entries), f32),
            pltpu.VMEM((4, 2 * size_z, entries), bf16),
            pltpu.VMEM((4, 3 * max(size_x, size_y), entries), f32),
            pltpu.VMEM((blocks, 5 * entries), f32),
            pltpu.VMEM((LANES, 5 * entries), bf16),
            pltpu.VMEM((4, 2, 1, size_z), f32),
            pltpu.VMEM((4, 2, 1, size_z), f32),
            pltpu.VMEM((4, 8, entries), f32),
            pltpu.VMEM((4, 8, entries), f32),
            pltpu.VMEM((steps, blocks, 1, LANES), f32),
            pltpu.VMEM((steps, count, 1, LANES), f32),
            pltpu.SemaphoreType.DMA((13,)),
            pltpu.SemaphoreType.DMA,
            pltpu.SemaphoreType.DMA((2,)),
            pltpu.SemaphoreType.DMA((2 * steps, 4)),
            pltpu.SemaphoreType.DMA((2 * steps, 4)),
            pltpu.SemaphoreType.DMA((4,)),
            pltpu.SemaphoreType.DMA((4,)),
            pltpu.SemaphoreType.DMA((4,)),
            pltpu.SemaphoreType.DMA((4,)),
            pltpu.SemaphoreType.DMA((steps,)),
            pltpu.SemaphoreType.DMA((steps,)),
        ],
        compiler_params=pltpu.CompilerParams(collective_id=0, has_side_effects=True),
        name="adjoint",
    )(*operands)
    state = pltpu.with_memory_space_constraint(state, pltpu.VMEM)
    slip = pltpu.with_memory_space_constraint(slip, pltpu.VMEM)
    return pl.pallas_call(
        put,
        out_shape=(
            jax.ShapeDtypeStruct(state.shape, f32),
            jax.ShapeDtypeStruct(slip.shape, f32),
        ),
        in_specs=[vmem, vmem],
        out_specs=(anywhere, anywhere),
        scratch_shapes=[pltpu.SemaphoreType.DMA((2,))],
        name="put",
    )(state, slip)


def solution(mesh):
    return jax.shard_map(
        shards,
        mesh=mesh,
        in_specs=(
            P(None, "strike", "dip", None),
            P("strike", "dip", None),
            P("strike", "dip", None),
            P("strike", "dip", None),
            P(("strike", "dip"), None, None),
            P(("strike", "dip"), None),
            P(("strike", "dip")),
            P(),
            P(("strike", "dip"), None),
            P(("strike", "dip"), None),
            P(("strike", "dip"), None),
            P(),
            P(),
        ),
        out_specs=(P(None, "strike", "dip", None), P(None, ("strike", "dip"))),
        check_vma=False,
    )
```

```python
import functools

import jax
import jax.numpy as jnp
from jax import lax
from jax.experimental import pallas as pl
from jax.experimental.pallas import tpu as pltpu
from jax.sharding import PartitionSpec as P

LANES = 128

time_step = 0.25

MESH = pl.DeviceIdType.MESH
NT_DIMS = (((1,), (1,)), ((), ()))


def split(x):
    high = x.astype(jnp.bfloat16)
    return high, (x - high.astype(jnp.float32)).astype(jnp.bfloat16)


def one_hot(shape, axis, ids):
    return jnp.where(lax.broadcasted_iota(jnp.int32, shape, axis) == ids, 1.0, 0.0).astype(jnp.bfloat16)


def matmul(a, b):
    return jnp.dot(a, b, preferred_element_type=jnp.float32)


def matmul_nt(a, b):
    return lax.dot_general(a, b, NT_DIMS, preferred_element_type=jnp.float32)


def along_x(f, low=None, high=None):
    low = jnp.zeros_like(f[0]) if low is None else low
    high = jnp.zeros_like(f[0]) if high is None else high
    before = jnp.concatenate([low[None], f[:-1]], axis=0)
    after = jnp.concatenate([f[1:], high[None]], axis=0)
    return (after - before) * 0.5


def along_y(f, low=0.0, high=0.0):
    size = f.shape[1]
    at = lax.broadcasted_iota(jnp.int32, f.shape, 1)
    before = jnp.where(at == 0, low, pltpu.roll(f, 1, 1))
    after = jnp.where(at == size - 1, high, pltpu.roll(f, size - 1, 1))
    return (after - before) * 0.5


def along_z(f):
    size = f.shape[2]
    at = lax.broadcasted_iota(jnp.int32, f.shape, 2)
    before = jnp.where(at == 0, 0.0, pltpu.roll(f, 1, 2))
    after = jnp.where(at == size - 1, 0.0, pltpu.roll(f, size - 1, 2))
    return (after - before) * 0.5


def both(x, axis):
    return jnp.concatenate(split(x), axis=axis)


def kernel(strike_count, dip_count, slot_count, *refs):
    far, refs = refs[:13], refs[13:]
    (out, slip), refs = refs[:2], refs[2:]
    near, refs = refs[:13], refs[13:]
    state, lam, mu, buoy, residual, tiles, cells, resample, patch, fault_cell, area, moment, order = near
    steps = resample.shape[0]
    turns = 2 * steps
    halves, refs = [refs[6 * t : 6 * t + 6] for t in range(turns)], refs[6 * turns :]
    (
        packed,
        landed,
        source,
        onehot_hi,
        pick,
        slope,
        face_pick,
        face_weight,
        block_hot,
        lane_hot,
        corner_out,
        corner_in,
        cross_out,
        cross_in,
        sums_out,
        sums_in,
        fetch_sem,
        route_send,
        route_recv,
        halo_send,
        halo_recv,
        corner_send,
        corner_recv,
        cross_send,
        cross_recv,
        sum_send,
        sum_recv,
    ) = refs
    count = strike_count * dip_count
    strike = lax.axis_index("strike")
    dip = lax.axis_index("dip")
    me = strike * dip_count + dip
    size_x, size_y, size_z = buoy.shape
    rows = size_x * size_y
    stations = residual.shape[1]
    entries = patch.shape[1]
    shift = size_z.bit_length() - 1
    group = LANES // slot_count
    value_rows = packed.shape[1]
    owned = order.shape[1] // count
    per_block = LANES // owned
    blocks = order.shape[1] // LANES
    half = 0.5 * time_step
    near_count = count // 2
    near_half = 2 * dip // dip_count
    here = dip * strike_count + strike
    halves_at = (near_half * near_count, (1 - near_half) * near_count)
    slots = near_count * slot_count

    flip_strike = strike < strike_count // 2
    flip_dip = dip < dip_count // 2

    def turned(flip, size, k):
        return jnp.where(flip, size - 1 - k, k)

    skip = turned(flip_dip, dip_count, dip) * strike_count + turned(flip_strike, strike_count, strike)

    def each_peer(act):
        def one(n, carry):
            at = n + jnp.where(n >= skip, 1, 0)
            to_strike = turned(flip_strike, strike_count, lax.rem(at, strike_count))
            to_dip = turned(flip_dip, dip_count, at // strike_count)
            act(to_strike * dip_count + to_dip, (to_strike, to_dip))
            return carry

        lax.fori_loop(0, count - 1, one, 0, unroll=count <= LANES)

    barrier = pltpu.get_barrier_semaphore()
    fetches = [pltpu.make_async_copy(far[i], near[i], fetch_sem.at[i]) for i in range(13)]
    early = (5, 6, 7, 4)
    each_peer(lambda to, device: pl.semaphore_signal(barrier, inc=1, device_id=device, device_id_type=MESH))

    for i in early:
        fetches[i].start()
    for i in range(13):
        if i not in early:
            fetches[i].start()

    sides = (
        (strike > 0, (strike - 1, dip)),
        (strike < strike_count - 1, (strike + 1, dip)),
        (dip > 0, (strike, dip - 1)),
        (dip < dip_count - 1, (strike, dip + 1)),
    )
    corners = tuple(
        (jnp.logical_and(sides[a][0], sides[2 + b][0]), (strike + 2 * a - 1, dip + 2 * b - 1))
        for a in range(2)
        for b in range(2)
    )

    def halo_copies(turn):
        x_out, x_low, x_high, y_out, y_low, y_high = halves[turn]
        copies = []
        for side in range(4):
            sender, low, high = (x_out, x_low, x_high) if side < 2 else (y_out, y_low, y_high)
            copies.append(
                pltpu.make_async_remote_copy(
                    src_ref=sender.at[side % 2],
                    dst_ref=high if side % 2 == 0 else low,
                    send_sem=halo_send.at[turn, side],
                    recv_sem=halo_recv.at[turn, side ^ 1],
                    device_id=sides[side][1],
                    device_id_type=MESH,
                )
            )
        return copies

    def corner_copies():
        return [
            pltpu.make_async_remote_copy(
                src_ref=corner_out.at[q],
                dst_ref=corner_in.at[3 - q],
                send_sem=corner_send.at[q],
                recv_sem=corner_recv.at[3 - q],
                device_id=corners[q][1],
                device_id_type=MESH,
            )
            for q in range(4)
        ]

    def cross_copies():
        return [
            pltpu.make_async_remote_copy(
                src_ref=cross_out.at[side],
                dst_ref=cross_in.at[side ^ 1],
                send_sem=cross_send.at[side],
                recv_sem=cross_recv.at[side ^ 1],
                device_id=sides[side][1],
                device_id_type=MESH,
            )
            for side in range(4)
        ]

    def received(turn, side):
        return halves[turn][(1, 2, 4, 5)[side]]

    def arrived(ref, sem):
        pltpu.make_async_copy(ref, ref, sem).wait()

    def stage(turn, at, x_face, y_face):
        x_out, y_out = halves[turn][0], halves[turn][3]
        for c in range(len(x_face)):
            f = x_face[c]
            x_out[0, at + c] = f[0]
            x_out[1, at + c] = f[size_x - 1]
            f = y_face[c]
            y_out[0, at + c] = f[:, 0:1]
            y_out[1, at + c] = f[:, size_y - 1 : size_y]

    def send(copies, where):
        for side, copy in enumerate(copies):
            pl.when(where[side][0])(copy.start)

    def receive(turn):
        for side in range(4):
            pl.when(sides[side][0])(functools.partial(arrived, received(turn, side), halo_recv.at[turn, side]))

    earlier = jnp.where(
        lax.broadcasted_iota(jnp.int32, (stations, stations), 0) < lax.broadcasted_iota(jnp.int32, (stations, stations), 1),
        1.0,
        0.0,
    ).astype(jnp.bfloat16)

    stress_x, stress_y = (3, 6, 7), (6, 4, 8)
    for i in early:
        fetches[i].wait()

    weights = both(resample[...] * time_step, 0)
    parts = [matmul_nt(weights, residual[c]) for c in range(3)]
    amplitude = [parts[c][k : k + 1] + parts[c][steps + k : steps + k + 1] for k in range(steps) for c in range(3)]
    cell_row = cells[...]
    hi_row = lax.shift_right_logical(cell_row, shift).astype(jnp.float32)
    lo_row = (cell_row & (size_z - 1)).astype(jnp.float32)
    values = jnp.concatenate(amplitude + [hi_row, lo_row], axis=0)
    named = one_hot((count, stations), 0, tiles[...])
    ordinal = jnp.sum(named.astype(jnp.float32) * matmul(named, earlier), axis=0, keepdims=True)
    slot_hot = lax.broadcasted_iota(jnp.int32, (slot_count, stations), 0) == ordinal.astype(jnp.int32)
    spread = []
    for r in range(value_rows):
        for part in split(values):
            pieces = [
                jnp.where(slot_hot, part[v : v + 1].astype(jnp.float32), 0.0)
                for v in range(r * group, min(8, (r + 1) * group))
            ]
            used = len(pieces) * slot_count
            if used < LANES:
                pieces.append(jnp.zeros((LANES - used, stations), jnp.float32))
            spread.append(jnp.concatenate(pieces, axis=0).astype(jnp.bfloat16))
    placed = matmul_nt(named, jnp.concatenate(spread, axis=0))
    for r in range(value_rows):
        at = 2 * r * LANES
        packed[:, r, :] = placed[:, at : at + LANES] + placed[:, at + LANES : at + 2 * LANES]

    pl.semaphore_wait(barrier, count - 1)

    def route(to, device):
        pltpu.make_async_remote_copy(
            src_ref=packed.at[to],
            dst_ref=landed.at[here],
            send_sem=route_send,
            recv_sem=route_recv.at[jnp.where(2 * device[1] // dip_count == near_half, 0, 1)],
            device_id=device,
            device_id_type=MESH,
        ).start()

    each_peer(route)
    landed[here] = packed[me]
    for i in (0, 1, 2):
        fetches[i].wait()
    stage(0, 0, [state[i] for i in stress_x], [state[i] for i in stress_y])
    stage(0, 3, [lam[...], mu[...]], [lam[...], mu[...]])
    send(halo_copies(0), sides)
    for i in range(3, 13):
        if i not in early:
            fetches[i].wait()

    for side in range(4):

        def clear(side=side):
            for turn in range(turns):
                target = received(turn, side)
                target[...] = jnp.zeros_like(target)
            cross_in[side] = jnp.zeros_like(cross_in[side])

        pl.when(jnp.logical_not(sides[side][0]))(clear)
    for q in range(4):

        def clear_corner(q=q):
            corner_in[q] = jnp.zeros_like(corner_in[q])

        pl.when(jnp.logical_not(corners[q][0]))(clear_corner)

    patch_row = patch[...]
    cell_e = fault_cell[...]
    row_e = lax.shift_right_logical(cell_e, shift)
    deep_e = cell_e & (size_z - 1)
    pick_lo = one_hot((size_z, entries), 0, deep_e)
    deep_iota = lax.broadcasted_iota(jnp.int32, (size_z, entries), 0)
    pick_slope = jnp.where(deep_iota == deep_e + 1, 1.0, jnp.where(deep_iota == deep_e - 1, -1.0, 0.0)).astype(jnp.bfloat16)
    pick_both = jnp.concatenate([pick_lo, pick_slope], axis=1)
    pick[...] = jnp.concatenate([pick_both, pick_both], axis=0)
    offset = lax.broadcasted_iota(jnp.int32, (rows, entries), 0) - row_e
    onehot_hi[...] = jnp.where(offset == 0, 1.0, 0.0)
    chosen = matmul(both(moment[...], 0), one_hot((moment.shape[1], entries), 0, patch_row))
    pattern = (chosen[:6] + chosen[6:]) * area[...]
    patch_col = jnp.transpose(jnp.broadcast_to(patch_row.astype(jnp.float32), (LANES, entries)))
    picks = jnp.concatenate(
        [
            jnp.where(patch_col == order[:, b * LANES : (b + 1) * LANES].astype(jnp.float32), 1.0, 0.0).astype(
                jnp.bfloat16
            )
            for b in range(blocks)
        ],
        axis=1,
    )
    number = lax.broadcasted_iota(jnp.int32, (8, order.shape[1]), 1)
    which = lax.broadcasted_iota(jnp.int32, (8, order.shape[1]), 0)
    number = jnp.where(which == 0, number // LANES, number % LANES).astype(jnp.float32).astype(jnp.bfloat16)
    place = matmul_nt(number, picks)[:2]

    def sampled(field):
        return matmul(both(field.reshape(rows, size_z), 1), pick[:, :entries])

    def at_entries(field):
        return jnp.sum(sampled(field) * onehot_hi[...], axis=0, keepdims=True)

    lam_e, mu_e = at_entries(lam[...]), at_entries(mu[...])
    stiff_e = lam_e + 2.0 * mu_e
    pxx, pyy, pzz, pxy, pxz, pyz = [pattern[m : m + 1] for m in range(6)]
    x_e, y_e = row_e // size_y, lax.rem(row_e, size_y)
    x_weight = (pxx * stiff_e + (pyy + pzz) * lam_e, pxy * mu_e, pxz * mu_e)
    y_weight = (pxy * mu_e, pyy * stiff_e + (pxx + pzz) * lam_e, pyz * mu_e)
    z_weight = (pxz * mu_e, pyz * mu_e, pzz * stiff_e + (pxx + pyy) * lam_e)
    for c in range(3):
        along, across, upward = half * x_weight[c], half * y_weight[c], half * z_weight[c]
        above = jnp.where(y_e < size_y - 1, across, 0.0)
        below = jnp.where(y_e > 0, -across, 0.0)
        grown = jnp.where(offset == size_y, along, jnp.where(offset == -size_y, -along, 0.0))
        slope[c, :, :entries] = jnp.where(offset == 1, above, jnp.where(offset == -1, below, grown))
        slope[c, :, entries:] = jnp.where(offset == 0, upward, 0.0)
    tail = [deep_e.astype(jnp.float32), place, jnp.zeros((1, entries), jnp.float32)]
    for side in range(4):
        on, across, weight = (x_e, y_e, x_weight) if side < 2 else (y_e, x_e, y_weight)
        edge = 0 if side % 2 == 0 else (size_x if side < 2 else size_y) - 1
        scale = jnp.where(on == edge, -half if side % 2 == 0 else half, 0.0)
        cross_out[side] = jnp.concatenate([w * scale for w in weight] + [across.astype(jnp.float32)] + tail, axis=0)
    send(cross_copies(), sides)

    def halo(turn, c):
        return [received(turn, side)[c] for side in range(4)]

    rhs = ((3, 6, 7), (6, 4, 8), (7, 8, 5))

    def velocity(fields, edges, extra):
        for c in range(3):
            xx, yy, zz = rhs[c]
            x_low, x_high, y_low, y_high = edges[c]
            total = along_x(fields[xx], x_low, x_high) + along_y(fields[yy], y_low, y_high) + along_z(fields[zz])
            moved = fields[c] + time_step * (buoy[...] * total)
            out[c] = moved if extra is None else moved + extra[c].reshape(size_x, size_y, size_z)

    def stress(old):
        lam_v, mu_v = lam[...], mu[...]
        vx, vy, vz = out[0], out[1], out[2]
        dxx, dyy, dzz = along_x(vx), along_y(vy), along_z(vz)
        bulk = lam_v * (dxx + dyy + dzz)
        out[3] = old[3] + time_step * (bulk + 2.0 * mu_v * dxx)
        out[4] = old[4] + time_step * (bulk + 2.0 * mu_v * dyy)
        out[5] = old[5] + time_step * (bulk + 2.0 * mu_v * dzz)
        scaled = time_step * mu_v
        out[6] = old[6] + scaled * (along_y(vx) + along_x(vy))
        out[7] = old[7] + scaled * (along_z(vx) + along_x(vz))
        out[8] = old[8] + scaled * (along_z(vy) + along_y(vz))

    def slope_x(f):
        zero = jnp.zeros_like(f[:1])
        return (jnp.concatenate([f[1:], zero], axis=0) - jnp.concatenate([zero, f[:-1]], axis=0)) * 0.5

    def slope_y(f):
        size = f.shape[0]
        at = lax.broadcasted_iota(jnp.int32, f.shape, 0)
        before = jnp.where(at == 0, 0.0, pltpu.roll(f, 1, 0))
        after = jnp.where(at == size - 1, 0.0, pltpu.roll(f, size - 1, 0))
        return (after - before) * 0.5

    def slope_z(f):
        axis = f.ndim - 1
        size = f.shape[axis]
        at = lax.broadcasted_iota(jnp.int32, f.shape, axis)
        before = jnp.where(at == 0, 0.0, pltpu.roll(f, 1, axis))
        after = jnp.where(at == size - 1, 0.0, pltpu.roll(f, size - 1, axis))
        return (after - before) * 0.5

    def stage_stress(turn, old):
        x_out, y_out = halves[turn][0], halves[turn][3]
        for side in range(2):
            i = (0, size_x - 1)[side]
            inner, sign = (1, 0.5) if side == 0 else (size_x - 2, -0.5)
            vx, vy, vz = [out[c, i] for c in range(3)]
            dx = [sign * out[c, inner] for c in range(3)]
            lam_v, mu_v = lam[i], mu[i]
            bulk = lam_v * (dx[0] + slope_y(vy) + slope_z(vz))
            x_out[side, 0] = old[3, i] + time_step * (bulk + 2.0 * mu_v * dx[0])
            x_out[side, 1] = old[6, i] + time_step * mu_v * (slope_y(vx) + dx[1])
            x_out[side, 2] = old[7, i] + time_step * mu_v * (slope_z(vx) + dx[2])
        for side in range(2):
            j = (0, size_y - 1)[side]
            inner, sign = (1, 0.5) if side == 0 else (size_y - 2, -0.5)
            at, near_at = slice(j, j + 1), slice(inner, inner + 1)
            vx, vy, vz = [out[c, :, at] for c in range(3)]
            dy = [sign * out[c, :, near_at] for c in range(3)]
            lam_v, mu_v = lam[:, at], mu[:, at]
            bulk = lam_v * (slope_x(vx) + dy[1] + slope_z(vz))
            y_out[side, 0] = old[6, :, at] + time_step * mu_v * (dy[0] + slope_x(vy))
            y_out[side, 1] = old[4, :, at] + time_step * (bulk + 2.0 * mu_v * dy[1])
            y_out[side, 2] = old[8, :, at] + time_step * mu_v * (slope_z(vy) + dy[2])

    def complete(turn):
        for side in range(4):
            sign = -half if side % 2 == 0 else half
            ex, ey, ez = [sign * received(turn, side)[c] for c in range(3)]
            if side < 2:
                i = 0 if side == 0 else size_x - 1
                lam_v, mu_v = lam[i], mu[i]
                bulk = lam_v * ex
                out[3, i] = out[3, i] + bulk + 2.0 * mu_v * ex
                out[4, i] = out[4, i] + bulk
                out[5, i] = out[5, i] + bulk
                out[6, i] = out[6, i] + mu_v * ey
                out[7, i] = out[7, i] + mu_v * ez
            else:
                at = pl.ds(0 if side == 2 else size_y - 1, 1)
                lam_v, mu_v = lam[:, at], mu[:, at]
                bulk = lam_v * ey
                out[3, :, at] = out[3, :, at] + bulk
                out[4, :, at] = out[4, :, at] + bulk + 2.0 * mu_v * ey
                out[5, :, at] = out[5, :, at] + bulk
                out[6, :, at] = out[6, :, at] + mu_v * ex
                out[8, :, at] = out[8, :, at] + mu_v * ez

    def stress_halo(turn):
        edges = []
        for side in range(4):
            ref = received(turn, side)
            lam_h, mu_h = received(0, side)[3], received(0, side)[4]
            sign = half if side % 2 == 0 else -half
            if side < 2:
                i = 0 if side == 0 else size_x - 1
                vx, vy, vz = [out[c, i] for c in range(3)]
                spot = lax.broadcasted_iota(jnp.int32, vx.shape, 0)
                ends = (corner_in.at[2 * side], corner_in.at[2 * side + 1])
                last = size_y - 1
            else:
                at = pl.ds(0 if side == 2 else size_y - 1, 1)
                vx, vy, vz = [out[c, :, at] for c in range(3)]
                spot = lax.broadcasted_iota(jnp.int32, vx.shape, 0)
                ends = (corner_in.at[side - 2], corner_in.at[side])
                last = size_x - 1

            def corner(c):
                return half * jnp.where(spot == 0, -ends[0][c], jnp.where(spot == last, ends[1][c], 0.0))

            stiff = sign * (lam_h + 2.0 * mu_h)
            if side < 2:
                first = ref[0] + stiff * vx + lam_h * corner(1)
                second = ref[1] + mu_h * (sign * vy + corner(0))
            else:
                first = ref[0] + mu_h * (sign * vx + corner(1))
                second = ref[1] + stiff * vy + lam_h * corner(0)
            edges.append((first, second, ref[2] + (sign * mu_h) * vz))
        return [[edges[side][c] for side in range(4)] for c in range(3)]

    def initial():
        total = None
        for m in range(6):
            taken = sampled(state[3 + m]) * pattern[m : m + 1]
            total = taken if total is None else total + taken
        return jnp.sum(total * onehot_hi[...], axis=0, keepdims=True)

    start_e = initial()

    def contribution():
        total = None
        for c in range(3):
            taken = matmul(both(out[c].reshape(rows, size_z), 1), pick[...]) * slope[c]
            taken = taken[:, :entries] + taken[:, entries:]
            total = taken if total is None else total + taken
        return jnp.sum(total, axis=0, keepdims=True)

    def face(side):
        if side < 2:
            i = 0 if side == 0 else size_x - 1
            return jnp.concatenate([out[c, i] for c in range(3)], axis=0)
        at = pl.ds(0 if side == 2 else size_y - 1, 1)
        return jnp.concatenate([out[c, :, at].reshape(size_x, size_z) for c in range(3)], axis=0)

    def crossing(side):
        f = face(side)
        felt = matmul(both(f, 1), face_pick[side]) * face_weight[side, : f.shape[0]]
        return jnp.sum(felt, axis=0, keepdims=True)

    def gather_sums(step, before):
        own = contribution()
        own = own if step else own + start_e
        pieces = jnp.concatenate([own] + [crossing(side) for side in range(4)], axis=1)
        high = pieces.astype(jnp.bfloat16).astype(jnp.float32)
        mask = block_hot[...]
        stacked = jnp.concatenate([mask * high, mask * (pieces - high)], axis=0).astype(jnp.bfloat16)
        total = matmul_nt(stacked, lane_hot[...])
        total = total[:blocks] + total[blocks:]
        total = total if before is None else before + total
        sums_out[:, step, :] = total
        return total

    def spread_sums():
        def one(to, device):
            pltpu.make_async_remote_copy(
                src_ref=sums_out.at[to // per_block],
                dst_ref=sums_in.at[me],
                send_sem=sum_send,
                recv_sem=sum_recv,
                device_id=device,
                device_id_type=MESH,
            ).start()

        each_peer(one)
        sums_in[me] = sums_out[me // per_block]

    def meet():
        for side in range(4):
            pl.when(sides[side][0])(functools.partial(arrived, cross_in.at[side], cross_recv.at[side]))
        place_hi, place_lo = [place[0:1]], [place[1:2]]
        for side in range(4):
            deep = cross_in[side, 4:5].astype(jnp.int32)
            chosen_deep = one_hot((size_z, entries), 0, deep)
            face_pick[side] = jnp.concatenate([chosen_deep, chosen_deep], axis=0)
            span = size_y if side < 2 else size_x
            on_row = lax.broadcasted_iota(jnp.int32, (span, entries), 0) == cross_in[side, 3:4].astype(jnp.int32)
            for c in range(3):
                face_weight[side, c * span : (c + 1) * span] = jnp.where(on_row, cross_in[side, c : c + 1], 0.0)
            place_hi.append(cross_in[side, 5:6])
            place_lo.append(cross_in[side, 6:7])
        place_hi = jnp.concatenate(place_hi, axis=1).astype(jnp.int32)
        place_lo = jnp.concatenate(place_lo, axis=1).astype(jnp.int32)
        block_hot[...] = jnp.where(lax.broadcasted_iota(jnp.int32, block_hot.shape, 0) == place_hi, 1.0, 0.0)
        lane_hot[...] = one_hot(lane_hot.shape, 0, place_lo)

    lane = lax.broadcasted_iota(jnp.int32, (slots // LANES, LANES), 1) // slot_count

    def unpacked(start):
        boxes = []
        high = slots // LANES
        for v in range(8):
            total = jnp.zeros((high, LANES), jnp.float32)
            for j in range(group):
                piece = landed[pl.ds(start + high * j, high), v // group, :]
                turn = ((j - v % group) * slot_count) % LANES
                total = jnp.where(lane == j, pltpu.roll(piece, turn, 1) if turn else piece, total)
            boxes.append(jnp.concatenate([total[i : i + 1] for i in range(high)], axis=1))
        inbox = jnp.concatenate(boxes, axis=0)
        spread_lo = one_hot((size_z, slots), 0, inbox[7:8].astype(jnp.int32))
        spread_lo = jnp.concatenate([spread_lo, spread_lo], axis=1)
        row_mask = lax.broadcasted_iota(jnp.int32, (rows, slots), 0) == inbox[6:7].astype(jnp.int32)
        amp_hi, amp_lo = split(inbox)
        return row_mask, spread_lo, amp_hi.astype(jnp.float32), amp_lo.astype(jnp.float32)

    def injected(box, m):
        row_mask, spread_lo, amp_hi, amp_lo = box
        high = jnp.where(row_mask, amp_hi[m : m + 1], 0.0).astype(jnp.bfloat16)
        low = jnp.where(row_mask, amp_lo[m : m + 1], 0.0).astype(jnp.bfloat16)
        return matmul_nt(jnp.concatenate([high, low], axis=1), spread_lo)

    arrived(landed.at[pl.ds(0, near_count - 1)], route_recv.at[0])
    box_near = unpacked(halves_at[0])
    first = [injected(box_near, c) for c in range(3)]
    receive(0)
    velocity(state, [halo(0, c) for c in range(3)], first)
    arrived(landed.at[pl.ds(0, near_count)], route_recv.at[1])
    box_far = unpacked(halves_at[1])
    for c in range(3):
        out[c] = out[c] + injected(box_far, c).reshape(size_x, size_y, size_z)

    total = None
    for step in range(steps):
        last = step == steps - 1
        turn = 2 * step + 1
        if step:
            receive(turn - 2)
            complete(turn - 2)
            receive(turn - 1)
            for q in range(4):
                pl.when(corners[q][0])(functools.partial(arrived, corner_in.at[q], corner_recv.at[q]))
            velocity(out, stress_halo(turn - 1), [source[(step - 1) * 3 + c] for c in range(3)])
        flow = [out[c] for c in range(3)]
        if last:
            gather_sums(step, total)
            spread_sums()
        else:
            for q in range(4):
                i, j = (0, size_x - 1)[q // 2], (0, size_y - 1)[q % 2]
                for c in range(2):
                    corner_out[q, c] = out[c, i, j : j + 1]
            send(corner_copies(), corners)
        stage(turn, 0, flow, flow)
        send(halo_copies(turn), sides)
        if not last:
            stage_stress(turn + 1, out if step else state)
            send(halo_copies(turn + 1), sides)
        stress(out if step else state)
        if not last:
            if step == 0:
                meet()
            for m in range(3):
                at = (step + 1) * 3 + m
                source[at - 3] = injected(box_near, at) + injected(box_far, at)
            total = gather_sums(step, total)
    receive(turns - 1)
    complete(turns - 1)

    arrived(landed.at[pl.ds(0, count - 1)], route_send)
    for turn in range(turns):
        for side, copy in enumerate(halo_copies(turn)):
            pl.when(sides[side][0])(copy.wait_send)
    for side, copy in enumerate(cross_copies()):
        pl.when(sides[side][0])(copy.wait_send)
    for q, copy in enumerate(corner_copies()):
        pl.when(corners[q][0])(copy.wait_send)
    all_sums = sums_in.at[pl.ds(0, count - 1)]
    arrived(all_sums, sum_send)
    arrived(all_sums, sum_recv)
    parts = [sums_in[t] for t in range(count)]
    while len(parts) > 1:
        parts = [a + b for a, b in zip(parts[::2], parts[1::2])]
    final = jnp.concatenate([parts[0], jnp.zeros((8 - steps, LANES), jnp.float32)], axis=0)
    first = lax.rem(me, per_block) * owned
    slip[...] = pltpu.roll(final, lax.rem(LANES - first, LANES), 1)[:steps, :owned]


def put(state, slip, out, grad, sems):
    copies = [pltpu.make_async_copy(state, out, sems.at[0]), pltpu.make_async_copy(slip, grad, sems.at[1])]
    for copy in copies:
        copy.start()
    for copy in copies:
        copy.wait()


def shards(
    adjoint_state,
    lame_lambda,
    lame_mu,
    buoyancy,
    residual,
    receiver_tile,
    receiver_cell,
    resample,
    fault_patch,
    fault_cell,
    fault_area,
    moment,
    subpatch_order,
):
    strike_count = lax.axis_size("strike")
    dip_count = lax.axis_size("dip")
    count = strike_count * dip_count
    stations = residual.shape[0]
    slot_count = max(2, (2 * stations + count - 1) // count)
    steps = resample.shape[0]
    size_x, size_y, size_z = buoyancy.shape
    rows = size_x * size_y
    group = LANES // slot_count
    value_rows = -(-8 // group)
    assert dip_count % 2 == 0 and count * slot_count % (2 * LANES) == 0 and group * slot_count == LANES
    entries = fault_patch.shape[1]
    patches = moment.shape[1]
    blocks = patches // LANES
    assert steps * 3 + 2 == 8
    anywhere = pl.BlockSpec(memory_space=pl.ANY)
    vmem = pl.BlockSpec(memory_space=pltpu.VMEM)
    f32, bf16 = jnp.float32, jnp.bfloat16
    operands = (
        adjoint_state,
        lame_lambda,
        lame_mu,
        buoyancy,
        jnp.swapaxes(residual, 0, 1),
        receiver_tile.reshape(1, stations),
        receiver_cell.reshape(1, stations),
        resample,
        fault_patch,
        fault_cell,
        fault_area,
        moment,
        subpatch_order.reshape(1, -1),
    )
    halves = []
    for fields in [5] + [3] * (2 * steps - 1):
        along, across = (fields, size_y, size_z), (fields, size_x, 1, size_z)
        halves += [pltpu.VMEM(shape, f32) for shape in ((2, *along), along, along, (2, *across), across, across)]
    state, slip = pl.pallas_call(
        functools.partial(kernel, strike_count, dip_count, slot_count),
        out_shape=(
            pltpu.VMEM(adjoint_state.shape, f32),
            pltpu.VMEM((steps, patches // count), f32),
        ),
        in_specs=[anywhere] * 13,
        out_specs=(vmem, vmem),
        scratch_shapes=[
            *(pltpu.VMEM(a.shape, a.dtype) for a in operands),
            *halves,
            pltpu.VMEM((count, value_rows, LANES), f32),
            pltpu.VMEM((count, value_rows, LANES), f32),
            pltpu.VMEM((steps * 3 - 3, rows, size_z), f32),
            pltpu.VMEM((rows, entries), f32),
            pltpu.VMEM((2 * size_z, 2 * entries), bf16),
            pltpu.VMEM((3, rows, 2 * entries), f32),
            pltpu.VMEM((4, 2 * size_z, entries), bf16),
            pltpu.VMEM((4, 3 * max(size_x, size_y), entries), f32),
            pltpu.VMEM((blocks, 5 * entries), f32),
            pltpu.VMEM((LANES, 5 * entries), bf16),
            pltpu.VMEM((4, 2, 1, size_z), f32),
            pltpu.VMEM((4, 2, 1, size_z), f32),
            pltpu.VMEM((4, 8, entries), f32),
            pltpu.VMEM((4, 8, entries), f32),
            pltpu.VMEM((blocks, steps, LANES), f32),
            pltpu.VMEM((count, steps, LANES), f32),
            pltpu.SemaphoreType.DMA((13,)),
            pltpu.SemaphoreType.DMA,
            pltpu.SemaphoreType.DMA((2,)),
            pltpu.SemaphoreType.DMA((2 * steps, 4)),
            pltpu.SemaphoreType.DMA((2 * steps, 4)),
            pltpu.SemaphoreType.DMA((4,)),
            pltpu.SemaphoreType.DMA((4,)),
            pltpu.SemaphoreType.DMA((4,)),
            pltpu.SemaphoreType.DMA((4,)),
            pltpu.SemaphoreType.DMA,
            pltpu.SemaphoreType.DMA,
        ],
        compiler_params=pltpu.CompilerParams(collective_id=0, has_side_effects=True),
        name="adjoint",
    )(*operands)
    state = pltpu.with_memory_space_constraint(state, pltpu.VMEM)
    slip = pltpu.with_memory_space_constraint(slip, pltpu.VMEM)
    return pl.pallas_call(
        put,
        out_shape=(
            jax.ShapeDtypeStruct(state.shape, f32),
            jax.ShapeDtypeStruct(slip.shape, f32),
        ),
        in_specs=[vmem, vmem],
        out_specs=(anywhere, anywhere),
        scratch_shapes=[pltpu.SemaphoreType.DMA((2,))],
        name="put",
    )(state, slip)


def solution(mesh):
    return jax.shard_map(
        shards,
        mesh=mesh,
        in_specs=(
            P(None, "strike", "dip", None),
            P("strike", "dip", None),
            P("strike", "dip", None),
            P("strike", "dip", None),
            P(("strike", "dip"), None, None),
            P(("strike", "dip"), None),
            P(("strike", "dip")),
            P(),
            P(("strike", "dip"), None),
            P(("strike", "dip"), None),
            P(("strike", "dip"), None),
            P(),
            P(),
        ),
        out_specs=(P(None, "strike", "dip", None), P(None, ("strike", "dip"))),
        check_vma=False,
    )
```
